32 devices in a mesh: groups: 2 (over y), attn: 4 (over x, core), exp: 4 (over z).
Axes of the slice: x: 2, y: 2, z: 4, core: 2. Of those that a mesh axis runs over, the one named last changes fastest.
Arguments:
- queries: bfloat16 [64, 32, 4096], P(('groups', 'exp'), None, 'attn'), parts along dimension 0, may hold values from -20 to 20
- new_keys: bfloat16 [64, 32, 512], P(('groups', 'exp'), None, 'attn'), parts along dimension 0, may hold values from -4 to 4
- new_values: bfloat16 [64, 32, 512], P(('groups', 'exp'), None, 'attn'), parts along dimension 0, may hold values from -4 to 4
- cache_keys: bfloat16 [64, 256, 512], P(('groups', 'exp'), None, 'attn'), parts along dimension 0, may hold values from -4 to 4
- cache_values: bfloat16 [64, 256, 512], P(('groups', 'exp'), None, 'attn'), parts along dimension 0, may hold values from -4 to 4
- cache_len: int32 [64], P(('groups', 'exp')), parts along dimension 0, may hold values from 2 to 256, as said below
- out_weight: bfloat16 [4096, 2048], P('attn', 'exp'), may hold values from -4 to 4
- residual: float32 [2048, 2048], P(('groups', 'exp', 'attn')), parts along dimension 0, may hold values from -6 to 6
- norm_gain: float32 [2048], replicated, may hold values from 0.1 to 1.9
- expert_ids: int32 [2048, 8], P(('groups', 'exp', 'attn')), parts along dimension 0, may hold values from 0 to 15, all different within a row; in each aligned block of 64 rows (0 to 63, 64 to 127, ...) at most 64 rows name the same one
- gate_nums: int32 [2048, 8], P(('groups', 'exp', 'attn')), parts along dimension 0, may hold values from 1 to 16
- w_gate_up: bfloat16 [16, 2048, 1536], P(('attn', 'exp')), may hold values from -0.125 to 0.125
- w_down: bfloat16 [16, 768, 2048], P(('attn', 'exp')), may hold values from -0.21875 to 0.21875
Outputs:
- mixed: float32 [2048, 2048], P(('groups', 'exp', 'attn')), parts along dimension 0
The draws below stay inside these ranges and needn't reach their ends.
There are 2 independent parts, one for each index of `groups`. The reference program is written for one: setup_inputs(seed, part) draws one part's arguments, and reference() takes and returns one part's arrays. A program takes and returns all parts, laid end to end along the dimension named above; an argument that names none is the same for every part. Nothing has to cross between parts.
Inputs may be any that keep to these rules, and one draw needn't show every extreme that they name: `cache_len`: number of valid cache slots of each session; some session has all 256. `expert_ids`: within the 64 rows of one device, no expert is named by more than 64 rows, and this bound is reached; each row names 8 distinct experts.
All inputs are finite; a program needn't handle non-finite values.
Results may differ from the reference program's by a relative error of at most 0.0038.
Values may be sent and summed in bfloat16 or wider, within the bound.
A program may use at most 128 MiB of HBM per device.

```python
import math
import jax
import jax.numpy as jnp
import numpy as np
from jax import lax

D = 2048
HEADS = 32
KVH = 4
HD = 128
MOE_FF = 768
TOP = 8
CACHE = 256
NEW = 32
SESSIONS = 32
TOKENS = 1024
TOK_DEV = 64
EXPERTS = 16
CAP = 64
N_ATTN = 4
N_EXP = 4


def shared_keys(key):
    keys = jnp.clip(jax.random.normal(jax.random.fold_in(key, 11), (SESSIONS, CACHE, KVH * HD), jnp.float32), -4.0, 4.0)
    return keys


def draw_cache_keys(key, part):
    keys = shared_keys(key)
    return keys.astype(jnp.bfloat16)


def draw_queries(key, part):
    base = jnp.clip(jax.random.normal(jax.random.fold_in(key, 21), (SESSIONS, NEW, HEADS * HD), jnp.float32), -4.0, 4.0)
    return base.astype(jnp.bfloat16)


def draw_cache_len(key, part):
    lengths = jax.random.randint(jax.random.fold_in(key, 31), (SESSIONS,), 2, CACHE + 1)
    where_full = jax.random.randint(jax.random.fold_in(key, 32), (), 0, SESSIONS)
    return jnp.where(jnp.arange(SESSIONS) == where_full, CACHE, lengths).astype(jnp.int32)


def touch_ends(drawn, rng, low, high):
    place = [jax.random.randint(jax.random.fold_in(rng, axis), (), 0, length) for axis, length in enumerate(drawn.shape)]
    longest = drawn.shape.index(max(drawn.shape))
    next_to = place[:longest] + [(place[longest] + 1) % drawn.shape[longest]] + place[longest + 1:]
    return drawn.at[tuple(place)].set(low).at[tuple(next_to)].set(high)


def shard_levels(stream_key, shape, pieces, least, top_value):
    level = 1.0
    for axis_at, parts in pieces:
        heights = jax.random.uniform(jax.random.fold_in(jax.random.fold_in(stream_key, 6), axis_at), (parts,), jnp.float32, least / len(pieces), top_value / len(pieces))
        level = level * jnp.repeat(jnp.exp(heights), shape[axis_at] // parts).reshape((-1,) + (1,) * (len(shape) - 1 - axis_at))
    return level


def routed_block(own_key, own, number, rows, number_of, top, reach, skew):
    ranking = jax.random.permutation(own_key, number_of)
    crowded, common = load_shares(number_of, rows * top, reach, skew, True), load_shares(number_of, rows * top, reach, skew, False)
    places = jnp.arange(number_of)

    def named(tallies, rotation):
        used = int((tallies > 0).sum())
        fixed = max(1, used // 4)
        shifted = fixed + (places - fixed + rotation * (used - fixed)) % max(1, number_of - fixed)
        return jnp.zeros((number_of,), jnp.int32).at[ranking[jnp.where(places < fixed, places, shifted)]].set(jnp.asarray(tallies, jnp.int32))

    tallies = jnp.where(number % 4 == 0, named(crowded, number // 4), named(common, number - number // 4 - 1))
    mixed = jax.random.permutation(jax.random.fold_in(own, 3), number_of)
    donor, taker = mixed[0:number_of // 2 * 2:2], mixed[1:number_of // 2 * 2:2]
    margin = jnp.minimum(tallies[donor] - 1, reach - tallies[taker]) // 2
    margin = jnp.where((donor == ranking[0]) | (taker == ranking[0]) | (tallies[taker] == 0), 0, jnp.maximum(margin, 0))
    shifted = jax.random.randint(jax.random.fold_in(own, 4), (number_of // 2,), 0, 1 << 20) % (margin + 1)
    tallies = tallies.at[donor].add(-shifted).at[taker].add(shifted)
    items = jnp.searchsorted(jnp.cumsum(tallies), jnp.arange(rows * top), side="right").astype(jnp.int32)
    table = items.reshape(top, rows).T
    table = table[jax.random.permutation(jax.random.fold_in(own, 1), rows)]
    rotation = jax.random.randint(jax.random.fold_in(own, 2), (rows, 1), 0, top)
    return jnp.take_along_axis(table, (jnp.arange(top)[None, :] + rotation) % top, axis=1)


def load_shares(amount, total, reach, slope, full):
    weights = [(1 << 20) // math.isqrt(rank ** slope) + 1 for rank in range(1, amount + 1)]
    largest = reach if full else min(reach, max(-(-total // amount), total * weights[0] // sum(weights)))
    least = 1 if total - largest >= amount - 1 else 0
    holding, surplus = [largest] + [least] * (amount - 1), total - largest - least * (amount - 1)
    while surplus > 0:
        free = [i for i in range(1, amount) if holding[i] < largest] or [i for i in range(1, amount) if holding[i] < reach]
        mass, budget = sum([weights[i] for i in free]), surplus
        for i in free:
            extra = min(reach - holding[i], max(1, budget * weights[i] // mass), surplus)
            holding[i] = holding[i] + extra
            surplus = surplus - extra
    return np.array(holding)


def noise(stream_key, dims, spread, limit, pieces=(), kind=jnp.bfloat16):
    entries = jax.random.normal(stream_key, dims, jnp.float32) * spread
    if len(pieces) > 0:
        entries = shard_levels(stream_key, dims, pieces, -0.22, 0.18) * entries
    return jnp.clip(entries, min=-limit, max=limit).astype(kind)


def setup_inputs(seed: int = 0, part: int = 0) -> dict:
    arg_keys = jax.random.split(jax.random.key(seed), 14)
    part_splits = jax.random.split(jax.random.fold_in(arg_keys[13], part), 14)
    queries = draw_queries(jax.random.fold_in(jax.random.fold_in(arg_keys[13], part), 71), part)
    new_keys = noise(part_splits[1], (SESSIONS, NEW, KVH * HD), 1.0, 4.0, ((0, 4), (2, 4)))
    new_values = noise(part_splits[2], (SESSIONS, NEW, KVH * HD), 1.0, 4.0, ((0, 4), (2, 4)))
    cache_keys = draw_cache_keys(jax.random.fold_in(jax.random.fold_in(arg_keys[13], part), 71), part)
    cache_values = noise(part_splits[4], (SESSIONS, CACHE, KVH * HD), 1.0, 4.0, ((0, 4), (2, 4)))
    cache_len = draw_cache_len(jax.random.fold_in(jax.random.fold_in(arg_keys[13], part), 71), part)
    out_weight = noise(arg_keys[6], (HEADS * HD, D), (16.0 * (HEADS * HD) ** -0.5), 4.0, ((0, 4), (1, 4)))
    residual = noise(part_splits[7], (TOKENS, D), 1.0, 6.0, ((0, 16),), jnp.float32)
    norm_gain = jnp.clip(1.0 + 0.18 * jax.random.normal(arg_keys[8], (D,), jnp.float32), 0.1, 1.9)
    expert_ids_keys = jax.random.split(jax.random.fold_in(part_splits[9], 1), TOKENS // TOK_DEV)
    expert_ids_turns = jax.random.permutation(jax.random.fold_in(part_splits[9], 3), TOKENS // TOK_DEV)
    expert_ids = jax.vmap(lambda own, number: routed_block(jax.random.fold_in(part_splits[9], 2), own, number, TOK_DEV, EXPERTS, TOP, CAP, 2))(expert_ids_keys, expert_ids_turns).reshape((TOKENS, TOP))
    gate_nums = touch_ends(jax.random.randint(part_splits[10], (TOKENS, TOP), 1, 17), jax.random.fold_in(part_splits[10], 1), 1, 16).astype(jnp.int32)
    w_gate_up = noise(arg_keys[11], (EXPERTS, D, 2 * MOE_FF), D ** -0.5, 0.125, ((0, 16),))
    w_down = noise(arg_keys[12], (EXPERTS, MOE_FF, D), MOE_FF ** -0.5, 0.21875, ((0, 16),))
    return {"queries": queries, "new_keys": new_keys, "new_values": new_values, "cache_keys": cache_keys, "cache_values": cache_values, "cache_len": cache_len, "out_weight": out_weight, "residual": residual, "norm_gain": norm_gain, "expert_ids": expert_ids, "gate_nums": gate_nums, "w_gate_up": w_gate_up, "w_down": w_down}


def attend_session(packed):
    q_s, k_new, v_new, k_old, v_old, length = packed
    n_new = q_s.shape[0]
    n_old = k_old.shape[0]
    kv_count = k_old.shape[-1] // HD
    group_size = q_s.shape[-1] // (kv_count * HD)
    q_four = q_s.astype(jnp.float32).reshape(n_new, kv_count, group_size, HD)
    k_old3 = k_old.astype(jnp.float32).reshape(n_old, kv_count, HD)
    v_old3 = v_old.astype(jnp.float32).reshape(n_old, kv_count, HD)
    k_new3 = k_new.astype(jnp.float32).reshape(n_new, kv_count, HD)
    v_new3 = v_new.astype(jnp.float32).reshape(n_new, kv_count, HD)
    scale = 1.0 / HD ** 0.5
    s_old = jnp.einsum('ikgd,jkd->kgij', q_four, k_old3) * scale
    s_new = jnp.einsum('ikgd,jkd->kgij', q_four, k_new3) * scale
    valid_old = jnp.arange(n_old, dtype=jnp.int32) < length
    s_old = jnp.where(valid_old[None, None, None, :], s_old, jnp.float32(-1e+30))
    causal = jnp.arange(n_new, dtype=jnp.int32)[None, :] <= jnp.arange(n_new, dtype=jnp.int32)[:, None]
    s_new = jnp.where(causal[None, None], s_new, jnp.float32(-1e+30))
    top = jnp.maximum(lax.optimization_barrier(jnp.max(s_old, -1, keepdims=True)), lax.optimization_barrier(jnp.max(s_new, -1, keepdims=True)))
    e_old = jnp.exp(s_old - top)
    e_new = jnp.exp(s_new - top)
    total = lax.optimization_barrier(jnp.sum(e_old, -1, keepdims=True)) + lax.optimization_barrier(jnp.sum(e_new, -1, keepdims=True))
    p_old = (e_old / total).astype(jnp.bfloat16).astype(jnp.float32)
    p_new = (e_new / total).astype(jnp.bfloat16).astype(jnp.float32)
    out = jnp.einsum('kgij,jkd->ikgd', p_old, v_old3) + jnp.einsum('kgij,jkd->ikgd', p_new, v_new3)
    return out.reshape(n_new, kv_count * group_size * HD).astype(jnp.bfloat16)

def run_expert(packed):
    block, gate_up, down = packed
    both = jnp.dot(block, gate_up, preferred_element_type=jnp.float32)
    hidden = (jax.nn.silu(both[:, :MOE_FF]) * both[:, MOE_FF:]).astype(jnp.bfloat16)
    return jnp.dot(hidden, down, preferred_element_type=jnp.float32).astype(jnp.bfloat16)

def reference(queries, new_keys, new_values, cache_keys, cache_values, cache_len, out_weight, residual, norm_gain, expert_ids, gate_nums, w_gate_up, w_down):
    attended = lax.map(attend_session, (queries, new_keys, new_values, cache_keys, cache_values, cache_len))
    flat = attended.reshape(TOKENS, HEADS * HD)
    middle = residual + jnp.dot(flat, out_weight, preferred_element_type=jnp.float32)
    meansq = lax.optimization_barrier(jnp.mean(middle * middle, -1, keepdims=True))
    normed = (middle * lax.rsqrt(meansq + 1e-06) * norm_gain).astype(jnp.bfloat16)
    n_dev = N_ATTN * N_EXP
    ids = expert_ids.reshape(n_dev, TOK_DEV * TOP)
    onehot = (ids[:, :, None] == jnp.arange(EXPERTS, dtype=jnp.int32)[None, None, :]).astype(jnp.int32)
    before = jnp.cumsum(onehot, axis=1) - onehot
    slot = lax.optimization_barrier(jnp.sum(before * onehot, -1)).astype(jnp.int32)
    source = jnp.arange(n_dev, dtype=jnp.int32)[:, None]
    index = ((ids * n_dev + source) * CAP + slot).reshape(-1).astype(jnp.int32)
    rows = jnp.broadcast_to(normed.reshape(TOKENS, 1, D), (TOKENS, TOP, D)).reshape(TOKENS * TOP, D)
    buffer = jnp.zeros((EXPERTS * n_dev * CAP, D), jnp.bfloat16).at[index].set(rows)
    outputs = lax.map(run_expert, (buffer.reshape(EXPERTS, n_dev * CAP, D), w_gate_up, w_down))
    picked = outputs.reshape(EXPERTS * n_dev * CAP, D)[index].reshape(TOKENS, TOP, D).astype(jnp.float32)
    numer = gate_nums.astype(jnp.float32)
    weights = numer / lax.optimization_barrier(jnp.sum(numer, -1, keepdims=True))
    return middle + lax.optimization_barrier(jnp.sum(picked * weights[:, :, None], 1))
```

```python
import jax
import jax.numpy as jnp
from jax import lax
from jax.experimental import pallas as pl
from jax.experimental.pallas import tpu as pltpu
from jax.sharding import PartitionSpec as P

HD = 128
LANES = 128
F32 = jnp.float32
BF16 = jnp.bfloat16


def places():
    g = lax.axis_index("groups")
    a = lax.axis_index("attn")
    z = lax.axis_index("exp")
    core = a + 1 - 2 * (a % 2)
    across = (a + 2) % 4
    planes = [z, z + 1 - 2 * (z % 2), (z + 2) % 4, 3 - z]
    inner = (z == 1) | (z == 2)
    return g, a, z, core, across, planes, inner


def meet(g, a, z, core, across, planes):
    barrier = pltpu.get_barrier_semaphore()
    peers = [(g, core, z), (g, across, z), (1 - g, a, z)] + [(g, a, p) for p in planes[1:]]
    for peer in peers:
        pl.semaphore_signal(barrier, inc=1, device_id=peer, device_id_type=pl.DeviceIdType.MESH)
    pl.semaphore_wait(barrier, len(peers))


def copy_to(src, dst, sems, i, j, where):
    return pltpu.make_async_remote_copy(
        src_ref=src,
        dst_ref=dst,
        send_sem=sems[0].at[i],
        recv_sem=sems[1].at[j],
        device_id=where,
        device_id_type=pl.DeviceIdType.MESH,
    )


def attend(q, k_new, v_new, k_old, v_old, length):
    n_new, n_old = q.shape[0], k_old.shape[0]
    kv_count = k_old.shape[1] // HD
    group = q.shape[1] // (kv_count * HD)
    scale = 1.0 / HD**0.5
    dims = (((1,), (1,)), ((), ()))
    heads = []
    for j in range(kv_count):
        cols = slice(j * HD, (j + 1) * HD)
        rows = jnp.concatenate(
            [q[:, (j * group + g) * HD : (j * group + g + 1) * HD] for g in range(group)], 0
        )
        s_old = lax.dot_general(rows, k_old[:, cols], dims, preferred_element_type=F32) * scale
        s_new = lax.dot_general(rows, k_new[:, cols], dims, preferred_element_type=F32) * scale
        valid = lax.broadcasted_iota(jnp.int32, s_old.shape, 1) < length
        s_old = jnp.where(valid, s_old, F32(-1e30))
        token = lax.broadcasted_iota(jnp.int32, (group, n_new, n_new), 1).reshape(s_new.shape)
        causal = lax.broadcasted_iota(jnp.int32, s_new.shape, 1) <= token
        s_new = jnp.where(causal, s_new, F32(-1e30))
        top = jnp.maximum(jnp.max(s_old, -1, keepdims=True), jnp.max(s_new, -1, keepdims=True))
        e_old = jnp.exp(s_old - top)
        e_new = jnp.exp(s_new - top)
        inv = 1.0 / (jnp.sum(e_old, -1, keepdims=True) + jnp.sum(e_new, -1, keepdims=True))
        p_old = (e_old * inv).astype(BF16)
        p_new = (e_new * inv).astype(BF16)
        out = jnp.dot(p_old, v_old[:, cols], preferred_element_type=F32)
        out = out + jnp.dot(p_new, v_new[:, cols], preferred_element_type=F32)
        out = out.astype(BF16)
        heads += [out[g * n_new : (g + 1) * n_new] for g in range(group)]
    return jnp.concatenate(heads, 1)


def layer_kernel(
    len_ref, q_hbm, kn_hbm, vn_hbm, kc_hbm, vc_hbm, wo_hbm, res_hbm, wgu_hbm, wd_hbm,
    gain_ref, ids_ref, gates_ref, out_ref,
    q_ref, kn_ref, vn_ref, kc_ref, vc_ref, wo_ref, wo_near, lsem, att,
    p_own, p_csend, p_crecv, p_xsend, p_xrecv, p_zsend, p_zrecv,
    a_s, a_r, w_s, w_r, p_s, p_r, pz_s, pz_r,
    wgu, wd, middle, wsem, xall, hid,
    own, csend, crecv, xsend, xrecv, zsend, zrecv,
    g_s, g_r, c_s, c_r, x_s, x_r, z_s, z_r,
):
    g, a, z, core, across, planes, inner = places()
    outer = jnp.logical_not(inner)
    opposite = (core + 2) % 4
    rows, width = out_ref.shape
    part = rows // 2
    n_new = q_ref.shape[1]
    cols = wo_ref.shape[1]
    heads = wo_ref.shape[0]
    units = wd.shape[0]
    mine = a * 4 + z
    half = width // 2
    w_rows = heads // 8

    at_core = (g, core, z)
    at_across = (g, across, z)
    at_group = (1 - g, a, z)

    def at_plane(k):
        return (g, a, planes[k])

    loads = [
        pltpu.make_async_copy(src, dst, lsem.at[i])
        for i, (src, dst) in enumerate(
            [
                (q_hbm, q_ref),
                (kn_hbm, kn_ref),
                (vn_hbm, vn_ref),
                (kc_hbm, kc_ref),
                (vc_hbm, vc_ref),
                (wo_hbm, wo_ref),
            ]
        )
    ]
    load_res = pltpu.make_async_copy(res_hbm, middle, wsem.at[2])
    load_gu = pltpu.make_async_copy(wgu_hbm.at[0], wgu, wsem.at[0])
    load_d = pltpu.make_async_copy(wd_hbm.at[0], wd, wsem.at[1])
    for load in loads + [load_res, load_gu, load_d]:
        load.start()
    meet(g, a, z, core, across, planes)

    expert = lax.broadcasted_iota(jnp.int32, (LANES, rows), 0)
    nums = jnp.zeros((LANES, rows), F32)
    for k in range(ids_ref.shape[0]):
        num = gates_ref[k : k + 1, :].astype(F32)
        nums = nums + jnp.where(expert == ids_ref[k : k + 1, :], num, F32(0))
    nums = nums.T.astype(BF16)
    for q in range(2):
        xall[q, 0, 0, :, width:] = nums[q * part : (q + 1) * part]
    for load in loads:
        load.wait()

    def att_copy(k_from, k_to, q, u, where):
        return copy_to(
            att.at[k_from, q, pl.ds(2 * u, 2)], att.at[k_to, q, pl.ds(2 * u, 2)],
            (a_s, a_r), k_from * 4 + 2 * q + u, k_to * 4 + 2 * q + u, where,
        )

    def att_out(q, u):
        step = inner.astype(jnp.int32)
        where = (g, a, planes[1] + step * (planes[3] - planes[1]))
        return att_copy(0, 1 + 2 * step, q, u, where)

    def att_wait(k, q, u):
        att_copy(0, k, q, u, at_plane(1)).wait_recv()

    def w_copy(p):
        rows_at = pl.ds(pl.multiple_of(g * (heads // 2) + p * w_rows, w_rows), w_rows)
        return copy_to(wo_ref.at[rows_at], wo_near.at[rows_at], (w_s, w_r), p, p, at_plane(1))

    def w_pass(p):
        rows_at = pl.ds(pl.multiple_of(g * (heads // 2) + p * w_rows, w_rows), w_rows)
        return copy_to(
            wo_near.at[rows_at], wo_near.at[rows_at], (w_s, w_r), 4 + p, 4 + p, at_group
        )

    def attention(q, u):
        for i in range(2):
            t = 4 * u + 2 * i + q
            att[0, q, 2 * u + i] = attend(
                q_ref[t], kn_ref[t], vn_ref[t], kc_ref[t], vc_ref[t], len_ref[t]
            )

    @pl.loop(0, 4)
    def _(j):
        q = j // 2
        u = j % 2
        attention(q, u)

        @pl.when(j < 2)
        def _():
            att_out(q, u).start()

        @pl.when((j == 1) & outer)
        def _():
            for p in range(4):
                w_copy(p).start()

    groups = [(0, 1), (1, 3), (3, 5)]

    def p_core(n, q):
        lo, hi = groups[n]
        return copy_to(
            p_csend.at[q, lo:hi], p_crecv.at[q, lo:hi], (p_s, p_r), 3 * q + n, 3 * q + n, at_core
        )

    def p_x(n, q):
        lo, hi = groups[n]
        i = 6 + 3 * q + n
        return copy_to(p_xsend.at[q, lo:hi], p_xrecv.at[q, lo:hi], (p_s, p_r), i, i, at_across)

    def p_z(k, q):
        i = 3 * q + k - 1
        return copy_to(p_zsend.at[q, k - 1], p_zrecv.at[q, k - 1], (pz_s, pz_r), i, i, at_plane(k))

    def att_rows(k, q):
        return jnp.concatenate(
            [att[k, q, a], att[k, q, across], att[k, q, core], att[k, q, opposite]], 0
        )

    def keep(job, q, r):
        p_own[q, job] = r[: 2 * part]
        p_csend[q, job] = r[2 * part :]

    def product_own(q):
        keep(0, q, jnp.dot(att_rows(0, q), wo_ref[...], preferred_element_type=F32))
        p_core(0, q).start()

    def product_near(q):
        keep(1, q, jnp.dot(att_rows(1, q), wo_ref[...], preferred_element_type=F32))
        keep(2, q, jnp.dot(att_rows(0, q), wo_near[...], preferred_element_type=F32))
        p_core(1, q).start()

    def product_far(q):
        x = jnp.concatenate([att_rows(2, q), att_rows(3, q)], 0)
        r = jnp.dot(x, wo_ref[...], preferred_element_type=F32)
        keep(3, q, r[: 4 * part])
        keep(4, q, r[4 * part :])
        p_core(2, q).start()

    def p_to_x(n, q):
        lo, hi = groups[n]
        p_core(n, q).wait_recv()
        for job in range(lo, hi):
            p_xsend[q, job] = (p_own[q, job, part:] + p_crecv[q, job, part:]).astype(BF16)
        p_x(n, q).start()

    def at_cols(k):
        return pl.ds(pl.multiple_of(planes[k] * cols, LANES), cols)

    def at_rows(q):
        return slice(q * part, (q + 1) * part)

    def p_total(job, q):
        return p_own[q, job, :part] + p_crecv[q, job, :part] + p_xrecv[q, job].astype(F32)

    def p_to_z(n, q):
        p_x(n, q).wait_recv()
        if n == 0:
            middle[at_rows(q), at_cols(0)] += p_total(0, q)
        if n == 1:
            p_zsend[q, 0] = p_total(1, q).astype(BF16)
            p_z(1, q).start()
            middle[at_rows(q), at_cols(1)] += p_total(2, q)
        if n == 2:
            for k in (2, 3):
                p_zsend[q, k - 1] = p_total(k + 1, q).astype(BF16)
                p_z(k, q).start()

    def p_take(k, q):
        p_z(k, q).wait_recv()
        middle[at_rows(q), at_cols(k)] += p_zrecv[q, k - 1].astype(F32)

    def normalise(q):
        @pl.when(outer)
        def _():
            p_take(1, q)

        p_take(2, q)
        p_take(3, q)
        m = middle[at_rows(q), :]
        meansq = jnp.mean(m * m, -1, keepdims=True)
        xall[q, 0, 0, :, :width] = (m * lax.rsqrt(meansq + 1e-06) * gain_ref[...]).astype(BF16)

    def rows_copy(q, s, ks, i_from, kd, i_to, where):
        return copy_to(
            xall.at[q, ks, i_from], xall.at[q, kd, i_to], (g_s, g_r),
            17 * q + s, 16 * q + 4 * kd + i_to, where,
        )

    def z_own(q, far):
        if far:
            return rows_copy(q, 1, 0, 0, 3, 0, at_plane(3))
        return rows_copy(q, 0, 0, 0, 1, 0, at_plane(1))

    def z_pass(q, k):
        kd = {1: 2, 3: 2, 2: 3}[k]
        return rows_copy(q, {1: 2, 3: 3, 2: 4}[k], k, 0, kd, 0, at_plane(3 if k == 1 else 1))

    def z_side(q):
        return rows_copy(q, 5, 0, 1, 1, 1, at_plane(1))

    def x_in(q, k):
        return rows_copy(q, {0: 6, 2: 7, 3: 8}[k], k, 0, k, 1, at_across)

    def core_in(q, k, i):
        return rows_copy(q, 9 + 2 * k + i, k, i, k, 2 + i, at_core)

    def gather_start(q):
        @pl.when(inner)
        def _():
            z_own(q, True).start()

        x_in(q, 0).start()
        z_own(q, False).start()
        core_in(q, 0, 0).start()

    def arrived(q, k, i):
        rows_copy(q, 0, 0, 0, k, i, at_plane(1)).wait_recv()

    def gather_near(q):
        arrived(q, 1, 0)

        @pl.when(inner)
        def _():
            z_pass(q, 1).start()

        core_in(q, 1, 0).start()
        arrived(q, 0, 1)
        z_side(q).start()
        core_in(q, 0, 1).start()

        @pl.when(inner)
        def _():
            arrived(q, 3, 0)
            z_pass(q, 3).start()
            x_in(q, 3).start()
            core_in(q, 3, 0).start()

        arrived(q, 1, 1)
        core_in(q, 1, 1).start()

    def gather_far(q):
        arrived(q, 2, 0)

        @pl.when(inner)
        def _():
            z_pass(q, 2).start()

        x_in(q, 2).start()
        core_in(q, 2, 0).start()

        @pl.when(outer)
        def _():
            arrived(q, 3, 0)
            x_in(q, 3).start()
            core_in(q, 3, 0).start()

        for k in (2, 3):
            arrived(q, k, 1)
            core_in(q, k, 1).start()

    def core_copy(q, b, h):
        i = 4 * q + 2 * b + h
        return copy_to(csend.at[q, b, h], crecv.at[q, b, h], (c_s, c_r), i, i, at_core)

    def x_copy(q, b, h):
        i = 4 * q + 2 * b + h
        return copy_to(xsend.at[q, b, h], xrecv.at[q, b, h], (x_s, x_r), i, i, at_across)

    def z_copy(q, k, h):
        i = 6 * q + 2 * (k - 1) + h
        return copy_to(zsend.at[q, k - 1, h], zrecv.at[q, k - 1, h], (z_s, z_r), i, i, at_plane(k))

    def compute(q, b, first=False):
        for k in (2 * b, 2 * b + 1):
            for i in (2, 3):
                arrived(q, k, i)
        if first:
            load_gu.wait()
        block = xall[q, 2 * b : 2 * b + 2].reshape(8 * part, width + LANES)
        x = block[:, :width]
        nums = block[:, width:].astype(F32)
        lane = lax.broadcasted_iota(jnp.int32, nums.shape, 1)
        num = jnp.sum(jnp.where(lane == mine, nums, F32(0)), -1, keepdims=True)
        weight = num / jnp.sum(nums, -1, keepdims=True)

        @pl.loop(0, units // 256)
        def _(t):
            at = pl.multiple_of(t * 256, 256)
            gate = jnp.dot(x, wgu[:, pl.ds(at, 256)], preferred_element_type=F32)
            up = jnp.dot(
                x,
                wgu[:, pl.ds(pl.multiple_of(units + t * 256, 256), 256)],
                preferred_element_type=F32,
            )
            hid[:, pl.ds(at, 256)] = (gate / (1.0 + jnp.exp(-gate)) * up).astype(BF16)

        if first:
            load_d.wait()

        for h in range(2):
            for t in range(2):
                lo = h * half + t * (half // 2)
                r = jnp.dot(hid[...], wd[:, lo : lo + half // 2], preferred_element_type=F32)
                r = r * weight
                at = slice(t * (half // 2), (t + 1) * (half // 2))
                for k in range(2):
                    own[q, b, h, k, :, at] = r[4 * k * part : (4 * k + 2) * part]
                    csend[q, b, h, k, :, at] = r[(4 * k + 2) * part : (4 * k + 4) * part].astype(
                        BF16
                    )
            core_copy(q, b, h).start()

    def to_x(q, b):
        for h in range(2):
            core_copy(q, b, h).wait_recv()
            total = own[q, b, h, :, part:, :] + crecv[q, b, h, :, part:, :].astype(F32)
            xsend[q, b, h] = total.astype(BF16)
            x_copy(q, b, h).start()

    def to_z(q, b):
        for h in range(2):
            x_copy(q, b, h).wait_recv()
            for k in range(2):
                total = own[q, b, h, k, :part, :] + crecv[q, b, h, k, :part, :].astype(F32)
                total = total + xrecv[q, b, h, k].astype(F32)
                plane = 2 * b + k
                if plane == 0:
                    at = slice(h * half, (h + 1) * half)
                    out_ref[at_rows(q), at] = middle[at_rows(q), at] + total
                else:
                    zsend[q, plane - 1, h] = total.astype(BF16)
                    z_copy(q, plane, h).start()

    def finish(q):
        for k in range(1, 4):
            for h in range(2):
                at = slice(h * half, (h + 1) * half)
                z_copy(q, k, h).wait_recv()
                out_ref[at_rows(q), at] += zrecv[q, k - 1, h].astype(F32)

    for q in range(2):
        product_own(q)

    @pl.when(inner)
    def _():
        for u in range(2):
            att_wait(3, 0, u)
            att_copy(3, 2, 0, u, at_plane(1)).start()
            att_wait(1, 0, u)
            att_copy(1, 2, 0, u, at_plane(3)).start()
        for u in range(2):
            att_out(1, u).start()
        for p in range(2):
            w_copy(p).wait_recv()
            w_pass(p).start()
        for u in range(2):
            att_wait(2, 0, u)
            att_copy(2, 3, 0, u, at_plane(1)).start()
        for p in range(2, 4):
            w_copy(p).wait_recv()
            w_pass(p).start()

    @pl.when(outer)
    def _():
        for p in range(2):
            w_copy(p).wait_send()
        for u in range(2):
            att_out(1, u).start()

    load_res.wait()
    for q in range(2):
        p_to_x(0, q)
    for q in range(2):
        p_to_z(0, q)

    def wait_far(q):
        @pl.when(outer)
        def _():
            for k in (2, 3):
                for u in range(2):
                    att_wait(k, q, u)

    wait_far(0)
    product_far(0)

    @pl.when(inner)
    def _():
        for p in range(4):
            w_pass(p).wait_recv()
        product_near(0)
        for u in range(2):
            att_wait(3, 1, u)
            att_copy(3, 2, 1, u, at_plane(1)).start()

    p_to_x(2, 0)

    @pl.when(inner)
    def _():
        p_to_x(1, 0)
        for u in range(2):
            att_wait(1, 1, u)
            att_copy(1, 2, 1, u, at_plane(3)).start()

    p_to_z(2, 0)

    @pl.when(inner)
    def _():
        p_to_z(1, 0)
        product_near(1)

    normalise(0)
    gather_start(0)

    @pl.when(inner)
    def _():
        for u in range(2):
            att_wait(2, 1, u)
            att_copy(2, 3, 1, u, at_plane(1)).start()
        p_to_x(1, 1)

    wait_far(1)
    product_far(1)
    gather_near(0)
    p_to_x(2, 1)

    @pl.when(inner)
    def _():
        p_to_z(1, 1)

    p_to_z(2, 1)
    normalise(1)
    gather_start(1)
    compute(0, 0, True)
    gather_far(0)
    to_x(0, 0)
    gather_near(1)
    compute(0, 1)
    to_z(0, 0)
    to_x(0, 1)
    compute(1, 0)
    gather_far(1)
    to_z(0, 1)
    to_x(1, 0)
    compute(1, 1)
    to_z(1, 0)
    to_x(1, 1)
    finish(0)
    to_z(1, 1)
    finish(1)

    for q in range(2):
        for u in range(2):
            att_out(q, u).wait_send()
        for n in (0, 2):
            p_core(n, q).wait_send()
            p_x(n, q).wait_send()
        for k in (2, 3):
            p_z(k, q).wait_send()
        z_own(q, False).wait_send()
        z_side(q).wait_send()
        for k in (0, 2, 3):
            x_in(q, k).wait_send()
        for k in range(4):
            for i in range(2):
                core_in(q, k, i).wait_send()
        for b in range(2):
            for h in range(2):
                core_copy(q, b, h).wait_send()
                x_copy(q, b, h).wait_send()
        for k in range(1, 4):
            for h in range(2):
                z_copy(q, k, h).wait_send()

    @pl.when(outer)
    def _():
        for p in range(2, 4):
            w_copy(p).wait_send()

    @pl.when(inner)
    def _():
        for p in range(4):
            w_pass(p).wait_send()
        for q in range(2):
            for u in range(2):
                att_copy(1, 2, q, u, at_plane(3)).wait_send()
                att_copy(3, 2, q, u, at_plane(1)).wait_send()
                att_copy(2, 3, q, u, at_plane(1)).wait_send()
            p_core(1, q).wait_send()
            p_x(1, q).wait_send()
            p_z(1, q).wait_send()
            z_own(q, True).wait_send()
            for k in (1, 2, 3):
                z_pass(q, k).wait_send()


def grid_shards(
    queries,
    new_keys,
    new_values,
    cache_keys,
    cache_values,
    cache_len,
    out_weight,
    residual,
    norm_gain,
    expert_ids,
    gate_nums,
    w_gate_up,
    w_down,
):
    rows, width = residual.shape
    units = w_down.shape[1]
    cols = out_weight.shape[1]
    heads = queries.shape[2]
    part = rows // 2
    half = width // 2
    vmem = pl.BlockSpec(memory_space=pltpu.VMEM)
    hbm = pl.BlockSpec(memory_space=pl.ANY)
    dma = pltpu.SemaphoreType.DMA
    return pl.pallas_call(
        layer_kernel,
        out_shape=jax.ShapeDtypeStruct((rows, width), F32),
        in_specs=[pl.BlockSpec(memory_space=pltpu.SMEM)] + [hbm] * 9 + [vmem] * 3,
        out_specs=vmem,
        scratch_shapes=[
            pltpu.VMEM(queries.shape, BF16),
            pltpu.VMEM(new_keys.shape, BF16),
            pltpu.VMEM(new_values.shape, BF16),
            pltpu.VMEM(cache_keys.shape, BF16),
            pltpu.VMEM(cache_values.shape, BF16),
            pltpu.VMEM(out_weight.shape, BF16),
            pltpu.VMEM(out_weight.shape, BF16),
            dma((6,)),
            pltpu.VMEM((4, 2, 4, part, heads), BF16),
            pltpu.VMEM((2, 5, 2 * part, cols), F32),
            pltpu.VMEM((2, 5, 2 * part, cols), F32),
            pltpu.VMEM((2, 5, 2 * part, cols), F32),
            pltpu.VMEM((2, 5, part, cols), BF16),
            pltpu.VMEM((2, 5, part, cols), BF16),
            pltpu.VMEM((2, 3, part, cols), BF16),
            pltpu.VMEM((2, 3, part, cols), BF16),
            dma((16,)),
            dma((16,)),
            dma((8,)),
            dma((8,)),
            dma((12,)),
            dma((12,)),
            dma((6,)),
            dma((6,)),
            pltpu.VMEM((width, 2 * units), BF16),
            pltpu.VMEM((units, width), BF16),
            pltpu.VMEM((rows, width), F32),
            dma((3,)),
            pltpu.VMEM((2, 4, 4, part, width + LANES), BF16),
            pltpu.VMEM((8 * part, units), BF16),
            pltpu.VMEM((2, 2, 2, 2, 2 * part, half), F32),
            pltpu.VMEM((2, 2, 2, 2, 2 * part, half), BF16),
            pltpu.VMEM((2, 2, 2, 2, 2 * part, half), BF16),
            pltpu.VMEM((2, 2, 2, 2, part, half), BF16),
            pltpu.VMEM((2, 2, 2, 2, part, half), BF16),
            pltpu.VMEM((2, 3, 2, part, half), BF16),
            pltpu.VMEM((2, 3, 2, part, half), BF16),
            dma((34,)),
            dma((32,)),
            dma((8,)),
            dma((8,)),
            dma((8,)),
            dma((8,)),
            dma((12,)),
            dma((12,)),
        ],
        compiler_params=pltpu.CompilerParams(
            collective_id=0, has_side_effects=True, vmem_limit_bytes=58 << 20
        ),
    )(
        cache_len, queries, new_keys, new_values, cache_keys, cache_values, out_weight,
        residual, w_gate_up, w_down, norm_gain.reshape(1, width), expert_ids.T, gate_nums.T,
    )


def attend_session(packed):
    q_s, k_new, v_new, k_old, v_old, length = packed
    n_new = q_s.shape[0]
    n_old = k_old.shape[0]
    kv_count = k_old.shape[-1] // HD
    group_size = q_s.shape[-1] // (kv_count * HD)
    q_four = q_s.reshape(n_new, kv_count, group_size, HD)
    k_old3 = k_old.reshape(n_old, kv_count, HD)
    v_old3 = v_old.reshape(n_old, kv_count, HD)
    k_new3 = k_new.reshape(n_new, kv_count, HD)
    v_new3 = v_new.reshape(n_new, kv_count, HD)
    scale = 1.0 / HD**0.5
    s_old = jnp.einsum("ikgd,jkd->kgij", q_four, k_old3, preferred_element_type=jnp.float32) * scale
    s_new = jnp.einsum("ikgd,jkd->kgij", q_four, k_new3, preferred_element_type=jnp.float32) * scale
    valid_old = jnp.arange(n_old, dtype=jnp.int32) < length
    s_old = jnp.where(valid_old[None, None, None, :], s_old, jnp.float32(-1e30))
    causal = (
        jnp.arange(n_new, dtype=jnp.int32)[None, :] <= jnp.arange(n_new, dtype=jnp.int32)[:, None]
    )
    s_new = jnp.where(causal[None, None], s_new, jnp.float32(-1e30))
    top = jnp.maximum(jnp.max(s_old, -1, keepdims=True), jnp.max(s_new, -1, keepdims=True))
    e_old = jnp.exp(s_old - top)
    e_new = jnp.exp(s_new - top)
    total = jnp.sum(e_old, -1, keepdims=True) + jnp.sum(e_new, -1, keepdims=True)
    p_old = (e_old / total).astype(jnp.bfloat16)
    p_new = (e_new / total).astype(jnp.bfloat16)
    out = jnp.einsum("kgij,jkd->ikgd", p_old, v_old3, preferred_element_type=jnp.float32)
    out = out + jnp.einsum("kgij,jkd->ikgd", p_new, v_new3, preferred_element_type=jnp.float32)
    return out.reshape(n_new, kv_count * group_size * HD).astype(jnp.bfloat16)


def shards(
    queries,
    new_keys,
    new_values,
    cache_keys,
    cache_values,
    cache_len,
    out_weight,
    residual,
    norm_gain,
    expert_ids,
    gate_nums,
    w_gate_up,
    w_down,
):
    attended = lax.map(
        attend_session, (queries, new_keys, new_values, cache_keys, cache_values, cache_len)
    )
    local_rows = attended.reshape(attended.shape[0] * attended.shape[1], attended.shape[2])
    spread = jnp.dot(
        lax.all_gather(local_rows, "exp", axis=0, tiled=True),
        out_weight,
        preferred_element_type=jnp.float32,
    )
    partial_value = lax.all_to_all(spread, "exp", split_axis=0, concat_axis=1, tiled=True)
    projected = lax.psum_scatter(partial_value, "attn", scatter_dimension=0, tiled=True)
    middle = residual + projected
    meansq = jnp.mean(middle * middle, -1, keepdims=True)
    normed = (middle * lax.rsqrt(meansq + 1e-06) * norm_gain).astype(jnp.bfloat16)
    tok_rows = expert_ids.shape[0]
    top_count = expert_ids.shape[1]
    exp_dev = w_gate_up.shape[0]
    hidden_units = w_down.shape[1]
    n_experts = exp_dev * lax.axis_size("attn") * lax.axis_size("exp")
    capacity = max(2, 2 * tok_rows * top_count // n_experts)
    flat_ids = expert_ids.reshape(-1)
    order = jnp.arange(flat_ids.shape[0], dtype=jnp.int32)
    earlier = (flat_ids[:, None] == flat_ids[None, :]) & (order[None, :] < order[:, None])
    slot = jnp.sum(earlier.astype(jnp.int32), -1)
    target = (flat_ids * capacity + slot).reshape(tok_rows, top_count)
    places = jnp.arange(n_experts * capacity, dtype=jnp.int32)
    placing = jnp.sum((places[:, None, None] == target[None, :, :]).astype(jnp.int32), -1).astype(
        jnp.bfloat16
    )
    sent = jnp.dot(placing, normed, preferred_element_type=jnp.float32).astype(jnp.bfloat16)
    sent = sent.reshape(n_experts, capacity, normed.shape[1])
    block = lax.all_to_all(sent, ("attn", "exp"), split_axis=0, concat_axis=0, tiled=True)
    n_src = block.shape[0] // exp_dev
    rows_four = block.reshape(n_src, exp_dev, block.shape[1], block.shape[2])
    both = jnp.einsum("sjmd,jdf->sjmf", rows_four, w_gate_up, preferred_element_type=jnp.float32)
    hidden = (jax.nn.silu(both[..., :hidden_units]) * both[..., hidden_units:]).astype(jnp.bfloat16)
    result = jnp.einsum("sjmf,jfd->sjmd", hidden, w_down, preferred_element_type=jnp.float32)
    result = result.astype(jnp.bfloat16).reshape(block.shape)
    returned = lax.all_to_all(result, ("attn", "exp"), split_axis=0, concat_axis=0, tiled=True)
    picked = (
        returned[flat_ids, slot].reshape(tok_rows, top_count, normed.shape[1]).astype(jnp.float32)
    )
    numer = gate_nums.astype(jnp.float32)
    weights = numer / jnp.sum(numer, -1, keepdims=True)
    return middle + jnp.sum(picked * weights[:, :, None], 1)


def fits_grid(mesh):
    return mesh.shape["groups"] == 2 and mesh.shape["attn"] == 4 and mesh.shape["exp"] == 4


def solution(mesh):
    in_specs = (
        P(("groups", "exp"), None, "attn"),
        P(("groups", "exp"), None, "attn"),
        P(("groups", "exp"), None, "attn"),
        P(("groups", "exp"), None, "attn"),
        P(("groups", "exp"), None, "attn"),
        P(("groups", "exp")),
        P("attn", "exp"),
        P(("groups", "exp", "attn"), None),
        P(),
        P(("groups", "exp", "attn"), None),
        P(("groups", "exp", "attn"), None),
        P(("attn", "exp"), None, None),
        P(("attn", "exp"), None, None),
    )
    out_specs = P(("groups", "exp", "attn"), None)
    body = grid_shards if fits_grid(mesh) else shards
    return jax.shard_map(body, mesh=mesh, in_specs=in_specs, out_specs=out_specs, check_vma=False)
```

```python
import jax
import jax.numpy as jnp
from jax import lax
from jax.experimental import pallas as pl
from jax.experimental.pallas import tpu as pltpu
from jax.sharding import PartitionSpec as P

HD = 128
LANES = 128
F32 = jnp.float32
BF16 = jnp.bfloat16


def places():
    g = lax.axis_index("groups")
    a = lax.axis_index("attn")
    z = lax.axis_index("exp")
    core = a + 1 - 2 * (a % 2)
    across = (a + 2) % 4
    planes = [z, z + 1 - 2 * (z % 2), (z + 2) % 4, 3 - z]
    inner = (z == 1) | (z == 2)
    return g, a, z, core, across, planes, inner


def meet(g, a, z, core, across, planes):
    barrier = pltpu.get_barrier_semaphore()
    peers = [(g, core, z), (g, across, z), (1 - g, a, z)] + [(g, a, p) for p in planes[1:]]
    for peer in peers:
        pl.semaphore_signal(barrier, inc=1, device_id=peer, device_id_type=pl.DeviceIdType.MESH)
    pl.semaphore_wait(barrier, len(peers))


def copy_to(src, dst, sems, i, j, where):
    return pltpu.make_async_remote_copy(
        src_ref=src,
        dst_ref=dst,
        send_sem=sems[0].at[i],
        recv_sem=sems[1].at[j],
        device_id=where,
        device_id_type=pl.DeviceIdType.MESH,
    )


def attend(q, k_new, v_new, k_old, v_old, length):
    n_new, n_old = q.shape[0], k_old.shape[0]
    kv_count = k_old.shape[1] // HD
    group = q.shape[1] // (kv_count * HD)
    scale = 1.0 / HD**0.5
    dims = (((1,), (1,)), ((), ()))
    heads = []
    for j in range(kv_count):
        cols = slice(j * HD, (j + 1) * HD)
        rows = jnp.concatenate(
            [q[:, (j * group + g) * HD : (j * group + g + 1) * HD] for g in range(group)], 0
        )
        s_old = lax.dot_general(rows, k_old[:, cols], dims, preferred_element_type=F32) * scale
        s_new = lax.dot_general(rows, k_new[:, cols], dims, preferred_element_type=F32) * scale
        valid = lax.broadcasted_iota(jnp.int32, s_old.shape, 1) < length
        s_old = jnp.where(valid, s_old, F32(-1e30))
        token = lax.broadcasted_iota(jnp.int32, (group, n_new, n_new), 1).reshape(s_new.shape)
        causal = lax.broadcasted_iota(jnp.int32, s_new.shape, 1) <= token
        s_new = jnp.where(causal, s_new, F32(-1e30))
        top = jnp.maximum(jnp.max(s_old, -1, keepdims=True), jnp.max(s_new, -1, keepdims=True))
        e_old = jnp.exp(s_old - top)
        e_new = jnp.exp(s_new - top)
        inv = 1.0 / (jnp.sum(e_old, -1, keepdims=True) + jnp.sum(e_new, -1, keepdims=True))
        p_old = (e_old * inv).astype(BF16)
        p_new = (e_new * inv).astype(BF16)
        out = jnp.dot(p_old, v_old[:, cols], preferred_element_type=F32)
        out = out + jnp.dot(p_new, v_new[:, cols], preferred_element_type=F32)
        out = out.astype(BF16)
        heads += [out[g * n_new : (g + 1) * n_new] for g in range(group)]
    return jnp.concatenate(heads, 1)


def layer_kernel(
    len_ref, q_hbm, kn_hbm, vn_hbm, kc_hbm, vc_hbm, wo_hbm, res_hbm, wgu_hbm, wd_hbm,
    gain_ref, ids_ref, gates_ref, out_ref,
    q_ref, kn_ref, vn_ref, kc_ref, vc_ref, wo_ref, wo_near, lsem, att,
    p_own, p_csend, p_crecv, p_xsend, p_xrecv, p_zsend, p_zrecv,
    a_s, a_r, w_s, w_r, p_s, p_r, pz_s, pz_r,
    wgu, wd, middle, wsem, xall, hid,
    own, csend, crecv, xsend, xrecv, zsend, zrecv,
    g_s, g_r, c_s, c_r, x_s, x_r, z_s, z_r,
):
    g, a, z, core, across, planes, inner = places()
    outer = jnp.logical_not(inner)
    opposite = (core + 2) % 4
    rows, width = out_ref.shape
    part = rows // 2
    cols = wo_ref.shape[1]
    heads = wo_ref.shape[0]
    units = wd.shape[0]
    mine = a * 4 + z
    half = width // 2
    w_rows = heads // 16

    at_core = (g, core, z)
    at_across = (g, across, z)
    at_group = (1 - g, a, z)

    def at_plane(k):
        return (g, a, planes[k])

    inner_int = inner.astype(jnp.int32)
    first_far = 2 + inner_int
    second_far = 3 - inner_int
    at_first = (g, a, planes[2] + inner_int * (planes[3] - planes[2]))
    at_second = (g, a, planes[3] + inner_int * (planes[2] - planes[3]))
    at_out = (g, a, planes[1] + inner_int * (planes[3] - planes[1]))
    out_slot = 1 + 2 * inner_int
    w_at = [
        pl.ds(pl.multiple_of(g * (heads // 2) + p * w_rows, w_rows), w_rows) for p in range(8)
    ]

    loads = [
        pltpu.make_async_copy(src, dst, lsem.at[i])
        for i, (src, dst) in enumerate(
            [
                (wo_hbm, wo_ref),
                (q_hbm, q_ref),
                (kn_hbm, kn_ref),
                (vn_hbm, vn_ref),
                (kc_hbm, kc_ref),
                (vc_hbm, vc_ref),
            ]
        )
    ]
    load_res = pltpu.make_async_copy(res_hbm, middle, wsem.at[2])
    load_gu = pltpu.make_async_copy(wgu_hbm.at[0], wgu, wsem.at[0])
    load_d = pltpu.make_async_copy(wd_hbm.at[0], wd, wsem.at[1])
    for load in loads + [load_res, load_gu, load_d]:
        load.start()
    meet(g, a, z, core, across, planes)

    def att_copy(k_from, k_to, q, u, where):
        return copy_to(
            att.at[k_from, q, u], att.at[k_to, q, u],
            (a_s, a_r), k_from * 8 + 4 * q + u, k_to * 8 + 4 * q + u, where,
        )

    def att_out(q, u):
        return att_copy(0, out_slot, q, u, at_out)

    def att_wait(k, q, u):
        att_copy(0, k, q, u, at_plane(1)).wait_recv()

    def w_copy(p):
        return copy_to(wo_ref.at[w_at[p]], wo_near.at[w_at[p]], (w_s, w_r), p, p, at_plane(1))

    def w_pass(p):
        return copy_to(
            wo_near.at[w_at[p]], wo_near.at[w_at[p]], (w_s, w_r), 8 + p, 8 + p, at_group
        )

    loads[0].wait()

    @pl.when(outer)
    def _():
        for p in range(3):
            w_copy(p).start()

    for load in loads[1:]:
        load.wait()

    @pl.loop(0, 8)
    def _(j):
        q = j // 4
        u = j % 4
        t = 2 * u + q
        att[0, q, u] = attend(q_ref[t], kn_ref[t], vn_ref[t], kc_ref[t], vc_ref[t], len_ref[t])

        @pl.when(j < 4)
        def _():
            att_out(q, u).start()

    groups = [(0, 1), (1, 3), (3, 4), (4, 5)]

    def p_core(n, q):
        lo, hi = groups[n]
        i = 4 * q + n
        return copy_to(p_csend.at[q, lo:hi], p_crecv.at[q, lo:hi], (p_s, p_r), i, i, at_core)

    def p_x(n, q):
        lo, hi = groups[n]
        i = 8 + 4 * q + n
        return copy_to(p_xsend.at[q, lo:hi], p_xrecv.at[q, lo:hi], (p_s, p_r), i, i, at_across)

    def p_z(n, q):
        k, where = {1: (1, at_plane(1)), 2: (first_far, at_first), 3: (second_far, at_second)}[n]
        return copy_to(
            p_zsend.at[q, n - 1], p_zrecv.at[q, k - 1], (pz_s, pz_r),
            3 * q + n - 1, 3 * q + k - 1, where,
        )

    def att_rows(k, q):
        return jnp.concatenate(
            [att[k, q, a], att[k, q, across], att[k, q, core], att[k, q, opposite]], 0
        )

    def keep(job, q, r):
        p_own[q, job] = r[: 2 * part]
        p_csend[q, job] = r[2 * part :]

    def product_own(q):
        keep(0, q, jnp.dot(att_rows(0, q), wo_ref[...], preferred_element_type=F32))
        p_core(0, q).start()

    def product_near(q):
        keep(1, q, jnp.dot(att_rows(1, q), wo_ref[...], preferred_element_type=F32))
        keep(2, q, jnp.dot(att_rows(0, q), wo_near[...], preferred_element_type=F32))
        p_core(1, q).start()

    def product_far(n, q):
        k = first_far if n == 2 else second_far
        keep(n + 1, q, jnp.dot(att_rows(k, q), wo_ref[...], preferred_element_type=F32))
        p_core(n, q).start()

    def p_to_x(n, q):
        lo, hi = groups[n]
        p_core(n, q).wait_recv()
        for job in range(lo, hi):
            p_xsend[q, job] = (p_own[q, job, part:] + p_crecv[q, job, part:]).astype(BF16)
        p_x(n, q).start()

    def at_cols(k):
        return pl.ds(pl.multiple_of(planes[k] * cols, LANES), cols)

    def at_rows(q):
        return slice(q * part, (q + 1) * part)

    def p_total(job, q):
        return p_own[q, job, :part] + p_crecv[q, job, :part] + p_xrecv[q, job].astype(F32)

    def p_to_z(n, q):
        p_x(n, q).wait_recv()
        if n == 0:
            middle[at_rows(q), at_cols(0)] += p_total(0, q)
        if n == 1:
            middle[at_rows(q), at_cols(1)] += p_total(2, q)
        if n > 0:
            p_zsend[q, n - 1] = p_total({1: 1, 2: 3, 3: 4}[n], q).astype(BF16)
            p_z(n, q).start()

    def p_take(k, q):
        copy_to(
            p_zsend.at[q, k - 1], p_zrecv.at[q, k - 1], (pz_s, pz_r),
            3 * q + k - 1, 3 * q + k - 1, at_plane(k),
        ).wait_recv()
        middle[at_rows(q), at_cols(k)] += p_zrecv[q, k - 1].astype(F32)

    def normalise(q, near):
        if near:
            p_take(1, q)
        p_take(2, q)
        p_take(3, q)
        m = middle[at_rows(q), :]
        meansq = jnp.mean(m * m, -1, keepdims=True)
        normed = (m * lax.rsqrt(meansq + 1e-06) * gain_ref[...]).astype(BF16)
        xall[q, 0, 0, :, :width] = normed

    def pass_att(k_from, k_to, q, u, plane):
        att_wait(k_from, q, u)
        att_copy(k_from, k_to, q, u, at_plane(plane)).start()

    def pass_w(p):
        w_copy(p).wait_recv()
        w_pass(p).start()

    def rows_copy(q, s, ks, i_from, kd, i_to, where):
        return copy_to(
            xall.at[q, ks, i_from], xall.at[q, kd, i_to], (g_s, g_r),
            17 * q + s, 16 * q + 4 * kd + i_to, where,
        )

    def z_own(q, far):
        if far:
            return rows_copy(q, 1, 0, 0, 3, 0, at_plane(3))
        return rows_copy(q, 0, 0, 0, 1, 0, at_plane(1))

    def z_pass(q, k):
        kd = {1: 2, 3: 2, 2: 3}[k]
        return rows_copy(q, {1: 2, 3: 3, 2: 4}[k], k, 0, kd, 0, at_plane(3 if k == 1 else 1))

    def x_in(q, k):
        return rows_copy(q, 5 + k, k, 0, k, 1, at_across)

    def core_in(q, k, i):
        return rows_copy(q, 9 + 2 * k + i, k, i, k, 2 + i, at_core)

    def gather_start(q, far):
        if far:
            z_own(q, True).start()
        x_in(q, 0).start()
        z_own(q, False).start()
        core_in(q, 0, 0).start()

    def arrived(q, k, i):
        rows_copy(q, 0, 0, 0, k, i, at_plane(1)).wait_recv()

    def pass_z(q, k, on):
        arrived(q, k, 0)
        if on:
            z_pass(q, k).start()
        x_in(q, k).start()
        core_in(q, k, 0).start()

    def pass_x(q, k):
        arrived(q, k, 1)
        core_in(q, k, 1).start()

    def gather_near(q):
        @pl.when(inner)
        def _():
            pass_z(q, 3, True)
            pass_z(q, 1, True)

        @pl.when(outer)
        def _():
            pass_z(q, 1, False)

    def gather_mid(q):
        @pl.when(inner)
        def _():
            pass_z(q, 2, True)

        @pl.when(outer)
        def _():
            pass_z(q, 2, False)

    def gather_far(q):
        @pl.when(outer)
        def _():
            pass_z(q, 3, False)

    def core_copy(q, b, h):
        i = 4 * q + 2 * b + h
        return copy_to(csend.at[q, b, h], crecv.at[q, b, h], (c_s, c_r), i, i, at_core)

    def x_copy(q, b, h):
        i = 4 * q + 2 * b + h
        return copy_to(xsend.at[q, b, h], xrecv.at[q, b, h], (x_s, x_r), i, i, at_across)

    def z_copy(q, k, h):
        i = 6 * q + 2 * (k - 1) + h
        return copy_to(zsend.at[q, k - 1, h], zrecv.at[q, k - 1, h], (z_s, z_r), i, i, at_plane(k))

    def compute(q, b, first=False):
        for k in (2 * b, 2 * b + 1):
            for i in (2, 3):
                arrived(q, k, i)
        if first:
            load_gu.wait()
        block = xall[q, 2 * b : 2 * b + 2].reshape(8 * part, width + LANES)
        x = block[:, :width]
        nums = block[:, width:].astype(F32)
        lane = lax.broadcasted_iota(jnp.int32, nums.shape, 1)
        num = jnp.sum(jnp.where(lane == mine, nums, F32(0)), -1, keepdims=True)
        weight = num / jnp.sum(nums, -1, keepdims=True)

        @pl.loop(0, units // 256)
        def _(t):
            at = pl.multiple_of(t * 256, 256)
            gate = jnp.dot(x, wgu[:, pl.ds(at, 256)], preferred_element_type=F32)
            up = jnp.dot(
                x,
                wgu[:, pl.ds(pl.multiple_of(units + t * 256, 256), 256)],
                preferred_element_type=F32,
            )
            hid[:, pl.ds(at, 256)] = (gate / (1.0 + jnp.exp(-gate)) * up).astype(BF16)

        if first:
            load_d.wait()

        for h in range(2):
            for t in range(2):
                lo = h * half + t * (half // 2)
                r = jnp.dot(hid[...], wd[:, lo : lo + half // 2], preferred_element_type=F32)
                r = r * weight
                at = slice(t * (half // 2), (t + 1) * (half // 2))
                for k in range(2):
                    own[q, b, h, k, :, at] = r[4 * k * part : (4 * k + 2) * part]
                    csend[q, b, h, k, :, at] = r[(4 * k + 2) * part : (4 * k + 4) * part].astype(
                        BF16
                    )
            core_copy(q, b, h).start()

    def to_x(q, b):
        for h in range(2):
            core_copy(q, b, h).wait_recv()
            total = own[q, b, h, :, part:, :] + crecv[q, b, h, :, part:, :].astype(F32)
            xsend[q, b, h] = total.astype(BF16)
            x_copy(q, b, h).start()

    def to_z(q, b):
        for h in range(2):
            x_copy(q, b, h).wait_recv()
            for k in range(2):
                total = own[q, b, h, k, :part, :] + crecv[q, b, h, k, :part, :].astype(F32)
                total = total + xrecv[q, b, h, k].astype(F32)
                plane = 2 * b + k
                if plane == 0:
                    at = slice(h * half, (h + 1) * half)
                    out_ref[at_rows(q), at] = middle[at_rows(q), at] + total
                else:
                    zsend[q, plane - 1, h] = total.astype(BF16)
                    z_copy(q, plane, h).start()

    def finish(q):
        for k in range(1, 4):
            for h in range(2):
                at = slice(h * half, (h + 1) * half)
                z_copy(q, k, h).wait_recv()
                out_ref[at_rows(q), at] += zrecv[q, k - 1, h].astype(F32)

    expert = lax.broadcasted_iota(jnp.int32, (LANES, rows), 0)
    nums = jnp.zeros((LANES, rows), F32)
    for k in range(ids_ref.shape[0]):
        num = gates_ref[k : k + 1, :].astype(F32)
        nums = nums + jnp.where(expert == ids_ref[k : k + 1, :], num, F32(0))
    nums = nums.T.astype(BF16)
    for q in range(2):
        xall[q, 0, 0, :, width:] = nums[at_rows(q)]
    load_res.wait()

    @pl.when(outer)
    def _():
        for u in range(4):
            att_out(0, u).wait_send()
            w_copy(3 + u).start()
        product_own(0)
        product_own(1)
        for u in range(4):
            att_wait(2, 0, u)
        product_far(2, 0)
        w_copy(3).wait_send()
        w_copy(7).start()
        p_to_x(0, 0)
        p_to_x(0, 1)
        w_copy(4).wait_send()
        att_out(1, 0).start()
        p_to_x(2, 0)
        for u in range(3):
            w_copy(5 + u).wait_send()
            att_out(1, 1 + u).start()
        p_to_z(0, 0)
        p_to_z(0, 1)
        p_to_z(2, 0)
        for u in range(4):
            att_wait(3, 0, u)
        product_far(3, 0)
        p_to_x(3, 0)
        for u in range(4):
            att_wait(2, 1, u)
        product_far(2, 1)
        p_to_z(3, 0)
        p_to_x(2, 1)
        normalise(0, True)
        gather_start(0, False)
        for u in range(4):
            att_wait(3, 1, u)
        product_far(3, 1)
        p_to_z(2, 1)
        p_to_x(3, 1)
        pass_z(0, 1, False)
        pass_x(0, 0)
        p_to_z(3, 1)
        pass_z(0, 2, False)
        normalise(1, True)
        gather_start(1, False)

    @pl.when(inner)
    def _():
        for u in range(4):
            pass_att(3, 2, 0, u, 1)
        for p in range(3):
            pass_w(p)
        for u in range(4):
            pass_att(1, 2, 0, u, 3)
            att_out(1, u).start()
        product_own(0)
        product_own(1)
        product_far(2, 0)
        for u in range(2):
            pass_att(2, 3, 0, u, 1)
        p_to_x(0, 0)
        p_to_x(0, 1)
        p_to_x(2, 0)
        pass_w(3)
        for u in range(2, 4):
            pass_att(2, 3, 0, u, 1)
        pass_w(4)
        product_far(3, 0)
        pass_w(5)
        p_to_z(0, 0)
        p_to_z(0, 1)
        p_to_z(2, 0)
        pass_w(6)
        p_to_x(3, 0)
        pass_w(7)
        for u in range(4):
            pass_att(3, 2, 1, u, 1)
        p_to_z(3, 0)
        pass_att(1, 2, 1, 0, 3)
        for p in range(8):
            w_pass(p).wait_recv()
        product_near(0)
        for u in range(1, 4):
            pass_att(1, 2, 1, u, 3)
        p_to_x(1, 0)
        product_far(2, 1)
        for u in range(2):
            pass_att(2, 3, 1, u, 1)
        p_to_x(2, 1)
        p_to_z(1, 0)
        normalise(0, False)
        gather_start(0, True)
        product_near(1)
        for u in range(2, 4):
            pass_att(2, 3, 1, u, 1)
        p_to_x(1, 1)
        product_far(3, 1)
        p_to_z(2, 1)
        p_to_x(3, 1)
        p_to_z(1, 1)
        pass_z(0, 3, True)
        pass_z(0, 1, True)
        pass_x(0, 0)
        p_to_z(3, 1)
        pass_z(0, 2, True)
        normalise(1, False)
        gather_start(1, True)

    pass_x(0, 1)
    compute(0, 0, True)
    gather_far(0)
    gather_near(1)
    pass_x(1, 0)
    to_x(0, 0)
    for k in (2, 3):
        pass_x(0, k)
    gather_mid(1)
    compute(0, 1)
    gather_far(1)
    pass_x(1, 1)
    to_x(0, 1)
    compute(1, 0)
    to_z(0, 0)
    for k in (2, 3):
        pass_x(1, k)
    to_x(1, 0)
    compute(1, 1)
    to_z(0, 1)
    to_x(1, 1)
    to_z(1, 0)
    finish(0)
    to_z(1, 1)
    finish(1)

    for q in range(2):
        for n in (0, 2, 3):
            p_core(n, q).wait_send()
            p_x(n, q).wait_send()
            if n > 0:
                p_z(n, q).wait_send()
        z_own(q, False).wait_send()
        for k in range(4):
            x_in(q, k).wait_send()
            for i in range(2):
                core_in(q, k, i).wait_send()
        for b in range(2):
            for h in range(2):
                core_copy(q, b, h).wait_send()
                x_copy(q, b, h).wait_send()
        for k in range(1, 4):
            for h in range(2):
                z_copy(q, k, h).wait_send()

    @pl.when(outer)
    def _():
        for u in range(4):
            att_out(1, u).wait_send()
        for p in range(3):
            w_copy(p).wait_send()

    @pl.when(inner)
    def _():
        for p in range(8):
            w_pass(p).wait_send()
        for q in range(2):
            for u in range(4):
                att_out(q, u).wait_send()
                att_copy(1, 2, q, u, at_plane(3)).wait_send()
                att_copy(3, 2, q, u, at_plane(1)).wait_send()
                att_copy(2, 3, q, u, at_plane(1)).wait_send()
            p_core(1, q).wait_send()
            p_x(1, q).wait_send()
            p_z(1, q).wait_send()
            z_own(q, True).wait_send()
            for k in range(1, 4):
                z_pass(q, k).wait_send()


def grid_shards(
    queries,
    new_keys,
    new_values,
    cache_keys,
    cache_values,
    cache_len,
    out_weight,
    residual,
    norm_gain,
    expert_ids,
    gate_nums,
    w_gate_up,
    w_down,
):
    rows, width = residual.shape
    units = w_down.shape[1]
    cols = out_weight.shape[1]
    heads = queries.shape[2]
    part = rows // 2
    half = width // 2
    vmem = pl.BlockSpec(memory_space=pltpu.VMEM)
    hbm = pl.BlockSpec(memory_space=pl.ANY)
    dma = pltpu.SemaphoreType.DMA
    return pl.pallas_call(
        layer_kernel,
        out_shape=jax.ShapeDtypeStruct((rows, width), F32),
        in_specs=[pl.BlockSpec(memory_space=pltpu.SMEM)] + [hbm] * 9 + [vmem] * 3,
        out_specs=vmem,
        scratch_shapes=[
            pltpu.VMEM(queries.shape, BF16),
            pltpu.VMEM(new_keys.shape, BF16),
            pltpu.VMEM(new_values.shape, BF16),
            pltpu.VMEM(cache_keys.shape, BF16),
            pltpu.VMEM(cache_values.shape, BF16),
            pltpu.VMEM(out_weight.shape, BF16),
            pltpu.VMEM(out_weight.shape, BF16),
            dma((6,)),
            pltpu.VMEM((4, 2, 4, part, heads), BF16),
            pltpu.VMEM((2, 5, 2 * part, cols), F32),
            pltpu.VMEM((2, 5, 2 * part, cols), F32),
            pltpu.VMEM((2, 5, 2 * part, cols), F32),
            pltpu.VMEM((2, 5, part, cols), BF16),
            pltpu.VMEM((2, 5, part, cols), BF16),
            pltpu.VMEM((2, 3, part, cols), BF16),
            pltpu.VMEM((2, 3, part, cols), BF16),
            dma((32,)),
            dma((32,)),
            dma((16,)),
            dma((16,)),
            dma((16,)),
            dma((16,)),
            dma((6,)),
            dma((6,)),
            pltpu.VMEM((width, 2 * units), BF16),
            pltpu.VMEM((units, width), BF16),
            pltpu.VMEM((rows, width), F32),
            dma((3,)),
            pltpu.VMEM((2, 4, 4, part, width + LANES), BF16),
            pltpu.VMEM((8 * part, units), BF16),
            pltpu.VMEM((2, 2, 2, 2, 2 * part, half), F32),
            pltpu.VMEM((2, 2, 2, 2, 2 * part, half), BF16),
            pltpu.VMEM((2, 2, 2, 2, 2 * part, half), BF16),
            pltpu.VMEM((2, 2, 2, 2, part, half), BF16),
            pltpu.VMEM((2, 2, 2, 2, part, half), BF16),
            pltpu.VMEM((2, 3, 2, part, half), BF16),
            pltpu.VMEM((2, 3, 2, part, half), BF16),
            dma((34,)),
            dma((32,)),
            dma((8,)),
            dma((8,)),
            dma((8,)),
            dma((8,)),
            dma((12,)),
            dma((12,)),
        ],
        compiler_params=pltpu.CompilerParams(
            collective_id=0, has_side_effects=True, vmem_limit_bytes=58 << 20
        ),
    )(
        cache_len, queries, new_keys, new_values, cache_keys, cache_values, out_weight,
        residual, w_gate_up, w_down, norm_gain.reshape(1, width), expert_ids.T, gate_nums.T,
    )


def attend_session(packed):
    q_s, k_new, v_new, k_old, v_old, length = packed
    n_new = q_s.shape[0]
    n_old = k_old.shape[0]
    kv_count = k_old.shape[-1] // HD
    group_size = q_s.shape[-1] // (kv_count * HD)
    q_four = q_s.reshape(n_new, kv_count, group_size, HD)
    k_old3 = k_old.reshape(n_old, kv_count, HD)
    v_old3 = v_old.reshape(n_old, kv_count, HD)
    k_new3 = k_new.reshape(n_new, kv_count, HD)
    v_new3 = v_new.reshape(n_new, kv_count, HD)
    scale = 1.0 / HD**0.5
    s_old = jnp.einsum("ikgd,jkd->kgij", q_four, k_old3, preferred_element_type=jnp.float32) * scale
    s_new = jnp.einsum("ikgd,jkd->kgij", q_four, k_new3, preferred_element_type=jnp.float32) * scale
    valid_old = jnp.arange(n_old, dtype=jnp.int32) < length
    s_old = jnp.where(valid_old[None, None, None, :], s_old, jnp.float32(-1e30))
    causal = (
        jnp.arange(n_new, dtype=jnp.int32)[None, :] <= jnp.arange(n_new, dtype=jnp.int32)[:, None]
    )
    s_new = jnp.where(causal[None, None], s_new, jnp.float32(-1e30))
    top = jnp.maximum(jnp.max(s_old, -1, keepdims=True), jnp.max(s_new, -1, keepdims=True))
    e_old = jnp.exp(s_old - top)
    e_new = jnp.exp(s_new - top)
    total = jnp.sum(e_old, -1, keepdims=True) + jnp.sum(e_new, -1, keepdims=True)
    p_old = (e_old / total).astype(jnp.bfloat16)
    p_new = (e_new / total).astype(jnp.bfloat16)
    out = jnp.einsum("kgij,jkd->ikgd", p_old, v_old3, preferred_element_type=jnp.float32)
    out = out + jnp.einsum("kgij,jkd->ikgd", p_new, v_new3, preferred_element_type=jnp.float32)
    return out.reshape(n_new, kv_count * group_size * HD).astype(jnp.bfloat16)


def shards(
    queries,
    new_keys,
    new_values,
    cache_keys,
    cache_values,
    cache_len,
    out_weight,
    residual,
    norm_gain,
    expert_ids,
    gate_nums,
    w_gate_up,
    w_down,
):
    attended = lax.map(
        attend_session, (queries, new_keys, new_values, cache_keys, cache_values, cache_len)
    )
    local_rows = attended.reshape(attended.shape[0] * attended.shape[1], attended.shape[2])
    spread = jnp.dot(
        lax.all_gather(local_rows, "exp", axis=0, tiled=True),
        out_weight,
        preferred_element_type=jnp.float32,
    )
    partial_value = lax.all_to_all(spread, "exp", split_axis=0, concat_axis=1, tiled=True)
    projected = lax.psum_scatter(partial_value, "attn", scatter_dimension=0, tiled=True)
    middle = residual + projected
    meansq = jnp.mean(middle * middle, -1, keepdims=True)
    normed = (middle * lax.rsqrt(meansq + 1e-06) * norm_gain).astype(jnp.bfloat16)
    tok_rows = expert_ids.shape[0]
    top_count = expert_ids.shape[1]
    exp_dev = w_gate_up.shape[0]
    hidden_units = w_down.shape[1]
    n_experts = exp_dev * lax.axis_size("attn") * lax.axis_size("exp")
    capacity = max(2, 2 * tok_rows * top_count // n_experts)
    flat_ids = expert_ids.reshape(-1)
    order = jnp.arange(flat_ids.shape[0], dtype=jnp.int32)
    earlier = (flat_ids[:, None] == flat_ids[None, :]) & (order[None, :] < order[:, None])
    slot = jnp.sum(earlier.astype(jnp.int32), -1)
    target = (flat_ids * capacity + slot).reshape(tok_rows, top_count)
    places = jnp.arange(n_experts * capacity, dtype=jnp.int32)
    placing = jnp.sum((places[:, None, None] == target[None, :, :]).astype(jnp.int32), -1).astype(
        jnp.bfloat16
    )
    sent = jnp.dot(placing, normed, preferred_element_type=jnp.float32).astype(jnp.bfloat16)
    sent = sent.reshape(n_experts, capacity, normed.shape[1])
    block = lax.all_to_all(sent, ("attn", "exp"), split_axis=0, concat_axis=0, tiled=True)
    n_src = block.shape[0] // exp_dev
    rows_four = block.reshape(n_src, exp_dev, block.shape[1], block.shape[2])
    both = jnp.einsum("sjmd,jdf->sjmf", rows_four, w_gate_up, preferred_element_type=jnp.float32)
    hidden = (jax.nn.silu(both[..., :hidden_units]) * both[..., hidden_units:]).astype(jnp.bfloat16)
    result = jnp.einsum("sjmf,jfd->sjmd", hidden, w_down, preferred_element_type=jnp.float32)
    result = result.astype(jnp.bfloat16).reshape(block.shape)
    returned = lax.all_to_all(result, ("attn", "exp"), split_axis=0, concat_axis=0, tiled=True)
    picked = (
        returned[flat_ids, slot].reshape(tok_rows, top_count, normed.shape[1]).astype(jnp.float32)
    )
    numer = gate_nums.astype(jnp.float32)
    weights = numer / jnp.sum(numer, -1, keepdims=True)
    return middle + jnp.sum(picked * weights[:, :, None], 1)


def fits_grid(mesh):
    return mesh.shape["groups"] == 2 and mesh.shape["attn"] == 4 and mesh.shape["exp"] == 4


def solution(mesh):
    in_specs = (
        P(("groups", "exp"), None, "attn"),
        P(("groups", "exp"), None, "attn"),
        P(("groups", "exp"), None, "attn"),
        P(("groups", "exp"), None, "attn"),
        P(("groups", "exp"), None, "attn"),
        P(("groups", "exp")),
        P("attn", "exp"),
        P(("groups", "exp", "attn"), None),
        P(),
        P(("groups", "exp", "attn"), None),
        P(("groups", "exp", "attn"), None),
        P(("attn", "exp"), None, None),
        P(("attn", "exp"), None, None),
    )
    out_specs = P(("groups", "exp", "attn"), None)
    body = grid_shards if fits_grid(mesh) else shards
    return jax.shard_map(body, mesh=mesh, in_specs=in_specs, out_specs=out_specs, check_vma=False)
```

```python
import jax
import jax.numpy as jnp
from jax import lax
from jax.experimental import pallas as pl
from jax.experimental.pallas import tpu as pltpu
from jax.sharding import PartitionSpec as P

HD = 128
LANES = 128
F32 = jnp.float32
BF16 = jnp.bfloat16


def places():
    g = lax.axis_index("groups")
    a = lax.axis_index("attn")
    z = lax.axis_index("exp")
    core = a + 1 - 2 * (a % 2)
    across = (a + 2) % 4
    planes = [z, z + 1 - 2 * (z % 2), (z + 2) % 4, 3 - z]
    inner = (z == 1) | (z == 2)
    return g, a, z, core, across, planes, inner


def meet(g, a, z, core, across, planes):
    barrier = pltpu.get_barrier_semaphore()
    peers = [(g, core, z), (g, across, z), (1 - g, a, z)] + [(g, a, p) for p in planes[1:]]
    for peer in peers:
        pl.semaphore_signal(barrier, inc=1, device_id=peer, device_id_type=pl.DeviceIdType.MESH)
    pl.semaphore_wait(barrier, len(peers))


def copy_to(src, dst, sems, i, j, where):
    return pltpu.make_async_remote_copy(
        src_ref=src,
        dst_ref=dst,
        send_sem=sems[0].at[i],
        recv_sem=sems[1].at[j],
        device_id=where,
        device_id_type=pl.DeviceIdType.MESH,
    )


def attend(q, k_new, v_new, k_old, v_old, length):
    n_new, n_old = q.shape[0], k_old.shape[0]
    kv_count = k_old.shape[1] // HD
    group = q.shape[1] // (kv_count * HD)
    scale = 1.0 / HD**0.5
    dims = (((1,), (1,)), ((), ()))
    heads = []
    for j in range(kv_count):
        cols = slice(j * HD, (j + 1) * HD)
        rows = jnp.concatenate(
            [q[:, (j * group + g) * HD : (j * group + g + 1) * HD] for g in range(group)], 0
        )
        s_old = lax.dot_general(rows, k_old[:, cols], dims, preferred_element_type=F32) * scale
        s_new = lax.dot_general(rows, k_new[:, cols], dims, preferred_element_type=F32) * scale
        valid = lax.broadcasted_iota(jnp.int32, s_old.shape, 1) < length
        s_old = jnp.where(valid, s_old, F32(-1e30))
        token = lax.broadcasted_iota(jnp.int32, (group, n_new, n_new), 1).reshape(s_new.shape)
        causal = lax.broadcasted_iota(jnp.int32, s_new.shape, 1) <= token
        s_new = jnp.where(causal, s_new, F32(-1e30))
        top = jnp.maximum(jnp.max(s_old, -1, keepdims=True), jnp.max(s_new, -1, keepdims=True))
        e_old = jnp.exp(s_old - top)
        e_new = jnp.exp(s_new - top)
        inv = 1.0 / (jnp.sum(e_old, -1, keepdims=True) + jnp.sum(e_new, -1, keepdims=True))
        p_old = (e_old * inv).astype(BF16)
        p_new = (e_new * inv).astype(BF16)
        out = jnp.dot(p_old, v_old[:, cols], preferred_element_type=F32)
        out = out + jnp.dot(p_new, v_new[:, cols], preferred_element_type=F32)
        out = out.astype(BF16)
        heads += [out[g * n_new : (g + 1) * n_new] for g in range(group)]
    return jnp.concatenate(heads, 1)


def layer_kernel(
    len_ref, q_hbm, kn_hbm, vn_hbm, kc_hbm, vc_hbm, wo_hbm, res_hbm, wgu_hbm, wd_hbm,
    gain_ref, ids_ref, gates_ref, out_ref,
    q_ref, kn_ref, vn_ref, kc_ref, vc_ref, wo_ref, wo_near, lsem, att,
    p_own, p_csend, p_crecv, p_xsend, p_xrecv, p_zsend, p_zrecv,
    a_s, a_r, w_s, w_r, p_s, p_r, pz_s, pz_r,
    wgu, wd, middle, wsem, xall, hid,
    own, csend, crecv, xsend, xrecv, zsend, zrecv,
    g_s, g_r, c_s, c_r, x_s, x_r, z_s, z_r,
):
    g, a, z, core, across, planes, inner = places()
    outer = jnp.logical_not(inner)
    opposite = (core + 2) % 4
    rows, width = out_ref.shape
    part = rows // 2
    cols = wo_ref.shape[1]
    heads = wo_ref.shape[0]
    units = wd.shape[0]
    mine = a * 4 + z
    half = width // 2
    w_rows = heads // 16

    at_core = (g, core, z)
    at_across = (g, across, z)
    at_group = (1 - g, a, z)

    def at_plane(k):
        return (g, a, planes[k])

    inner_int = inner.astype(jnp.int32)
    first_far = 2 + inner_int
    second_far = 3 - inner_int
    at_first = (g, a, planes[2] + inner_int * (planes[3] - planes[2]))
    at_second = (g, a, planes[3] + inner_int * (planes[2] - planes[3]))
    at_out = (g, a, planes[1] + inner_int * (planes[3] - planes[1]))
    out_slot = 1 + 2 * inner_int
    w_at = [
        pl.ds(pl.multiple_of(g * (heads // 2) + p * w_rows, w_rows), w_rows) for p in range(8)
    ]

    loads = [
        pltpu.make_async_copy(src, dst, lsem.at[i])
        for i, (src, dst) in enumerate(
            [
                (wo_hbm, wo_ref),
                (q_hbm, q_ref),
                (kn_hbm, kn_ref),
                (vn_hbm, vn_ref),
                (kc_hbm, kc_ref),
                (vc_hbm, vc_ref),
            ]
        )
    ]
    load_res = pltpu.make_async_copy(res_hbm, middle, wsem.at[2])
    load_gu = pltpu.make_async_copy(wgu_hbm.at[0], wgu, wsem.at[0])
    load_d = pltpu.make_async_copy(wd_hbm.at[0], wd, wsem.at[1])
    for load in loads + [load_res, load_gu, load_d]:
        load.start()
    meet(g, a, z, core, across, planes)

    def att_copy(k_from, k_to, q, u, where):
        return copy_to(
            att.at[k_from, q, u], att.at[k_to, q, u],
            (a_s, a_r), k_from * 8 + 4 * q + u, k_to * 8 + 4 * q + u, where,
        )

    def att_out(q, u):
        return att_copy(0, out_slot, q, u, at_out)

    def att_wait(k, q, u):
        att_copy(0, k, q, u, at_plane(1)).wait_recv()

    def w_copy(p):
        return copy_to(wo_ref.at[w_at[p]], wo_near.at[w_at[p]], (w_s, w_r), p, p, at_plane(1))

    def w_pass(p):
        return copy_to(
            wo_near.at[w_at[p]], wo_near.at[w_at[p]], (w_s, w_r), 8 + p, 8 + p, at_group
        )

    loads[0].wait()

    @pl.when(outer)
    def _():
        for p in range(3):
            w_copy(p).start()

    for load in loads[1:]:
        load.wait()

    @pl.loop(0, 8)
    def _(j):
        q = j // 4
        u = j % 4
        t = 2 * u + q
        att[0, q, u] = attend(q_ref[t], kn_ref[t], vn_ref[t], kc_ref[t], vc_ref[t], len_ref[t])

        @pl.when(j < 4)
        def _():
            att_out(q, u).start()

    groups = [(0, 1), (1, 3), (3, 4), (4, 5)]

    def p_core(n, q):
        lo, hi = groups[n]
        i = 4 * q + n
        return copy_to(p_csend.at[q, lo:hi], p_crecv.at[q, lo:hi], (p_s, p_r), i, i, at_core)

    def p_x(n, q):
        lo, hi = groups[n]
        i = 8 + 4 * q + n
        return copy_to(p_xsend.at[q, lo:hi], p_xrecv.at[q, lo:hi], (p_s, p_r), i, i, at_across)

    def p_z(n, q):
        k, where = {1: (1, at_plane(1)), 2: (first_far, at_first), 3: (second_far, at_second)}[n]
        return copy_to(
            p_zsend.at[q, n - 1], p_zrecv.at[q, k - 1], (pz_s, pz_r),
            3 * q + n - 1, 3 * q + k - 1, where,
        )

    def att_rows(k, q):
        return jnp.concatenate(
            [att[k, q, a], att[k, q, across], att[k, q, core], att[k, q, opposite]], 0
        )

    def keep(job, q, r):
        p_own[q, job] = r[: 2 * part]
        p_csend[q, job] = r[2 * part :]

    def product_own(q):
        keep(0, q, jnp.dot(att_rows(0, q), wo_ref[...], preferred_element_type=F32))
        p_core(0, q).start()

    def product_near(q):
        keep(1, q, jnp.dot(att_rows(1, q), wo_ref[...], preferred_element_type=F32))
        keep(2, q, jnp.dot(att_rows(0, q), wo_near[...], preferred_element_type=F32))
        p_core(1, q).start()

    def product_far(n, q):
        k = first_far if n == 2 else second_far
        keep(n + 1, q, jnp.dot(att_rows(k, q), wo_ref[...], preferred_element_type=F32))
        p_core(n, q).start()

    def p_to_x(n, q):
        lo, hi = groups[n]
        p_core(n, q).wait_recv()
        for job in range(lo, hi):
            p_xsend[q, job] = (p_own[q, job, part:] + p_crecv[q, job, part:]).astype(BF16)
        p_x(n, q).start()

    def at_cols(k):
        return pl.ds(pl.multiple_of(planes[k] * cols, LANES), cols)

    def at_rows(q):
        return slice(q * part, (q + 1) * part)

    def p_total(job, q):
        return p_own[q, job, :part] + p_crecv[q, job, :part] + p_xrecv[q, job].astype(F32)

    def p_to_z(n, q):
        p_x(n, q).wait_recv()
        if n == 0:
            middle[at_rows(q), at_cols(0)] += p_total(0, q)
        if n == 1:
            middle[at_rows(q), at_cols(1)] += p_total(2, q)
        if n > 0:
            p_zsend[q, n - 1] = p_total({1: 1, 2: 3, 3: 4}[n], q).astype(BF16)
            p_z(n, q).start()

    def p_take(k, q):
        copy_to(
            p_zsend.at[q, k - 1], p_zrecv.at[q, k - 1], (pz_s, pz_r),
            3 * q + k - 1, 3 * q + k - 1, at_plane(k),
        ).wait_recv()
        middle[at_rows(q), at_cols(k)] += p_zrecv[q, k - 1].astype(F32)

    def normalise(q, near):
        if near:
            p_take(1, q)
        p_take(2, q)
        p_take(3, q)
        m = middle[at_rows(q), :]
        meansq = jnp.mean(m * m, -1, keepdims=True)
        normed = (m * lax.rsqrt(meansq + 1e-06) * gain_ref[...]).astype(BF16)
        xall[q, 0, 0, :, :width] = normed

    def pass_att(k_from, k_to, q, u, plane):
        att_wait(k_from, q, u)
        att_copy(k_from, k_to, q, u, at_plane(plane)).start()

    def pass_w(p):
        w_copy(p).wait_recv()
        w_pass(p).start()

    def rows_copy(q, s, ks, i_from, kd, i_to, where):
        return copy_to(
            xall.at[q, ks, i_from], xall.at[q, kd, i_to], (g_s, g_r),
            17 * q + s, 16 * q + 4 * kd + i_to, where,
        )

    def z_own(q, far):
        if far:
            return rows_copy(q, 1, 0, 0, 3, 0, at_plane(3))
        return rows_copy(q, 0, 0, 0, 1, 0, at_plane(1))

    def z_pass(q, k):
        kd = {1: 2, 3: 2, 2: 3}[k]
        return rows_copy(q, {1: 2, 3: 3, 2: 4}[k], k, 0, kd, 0, at_plane(3 if k == 1 else 1))

    def x_in(q, k):
        return rows_copy(q, 5 + k, k, 0, k, 1, at_across)

    def core_in(q, k, i):
        return rows_copy(q, 9 + 2 * k + i, k, i, k, 2 + i, at_core)

    def gather_start(q, far):
        if far:
            z_own(q, True).start()
        x_in(q, 0).start()
        z_own(q, False).start()
        core_in(q, 0, 0).start()

    def arrived(q, k, i):
        rows_copy(q, 0, 0, 0, k, i, at_plane(1)).wait_recv()

    def pass_z(q, k, on):
        arrived(q, k, 0)
        if on:
            z_pass(q, k).start()
        x_in(q, k).start()
        core_in(q, k, 0).start()

    def pass_x(q, k):
        arrived(q, k, 1)
        core_in(q, k, 1).start()

    def gather_near(q):
        @pl.when(inner)
        def _():
            pass_z(q, 3, True)
            pass_z(q, 1, True)

        @pl.when(outer)
        def _():
            pass_z(q, 1, False)

    def gather_mid(q):
        @pl.when(inner)
        def _():
            pass_z(q, 2, True)

        @pl.when(outer)
        def _():
            pass_z(q, 2, False)

    def gather_far(q):
        @pl.when(outer)
        def _():
            pass_z(q, 3, False)

    def core_copy(q, b, h):
        i = 4 * q + 2 * b + h
        return copy_to(csend.at[q, b, h], crecv.at[q, b, h], (c_s, c_r), i, i, at_core)

    def x_copy(q, b, h):
        i = 4 * q + 2 * b + h
        return copy_to(xsend.at[q, b, h], xrecv.at[q, b, h], (x_s, x_r), i, i, at_across)

    def z_copy(q, k, h):
        i = 6 * q + 2 * (k - 1) + h
        return copy_to(zsend.at[q, k - 1, h], zrecv.at[q, k - 1, h], (z_s, z_r), i, i, at_plane(k))

    def compute(q, b, first=False):
        for k in (2 * b, 2 * b + 1):
            for i in (2, 3):
                arrived(q, k, i)
        if first:
            load_gu.wait()
        block = xall[q, 2 * b : 2 * b + 2].reshape(8 * part, width + LANES)
        x = block[:, :width]
        nums = block[:, width:].astype(F32)
        lane = lax.broadcasted_iota(jnp.int32, nums.shape, 1)
        num = jnp.sum(jnp.where(lane == mine, nums, F32(0)), -1, keepdims=True)
        weight = num / jnp.sum(nums, -1, keepdims=True)

        @pl.loop(0, units // 256)
        def _(t):
            at = pl.multiple_of(t * 256, 256)
            gate = jnp.dot(x, wgu[:, pl.ds(at, 256)], preferred_element_type=F32)
            up = jnp.dot(
                x,
                wgu[:, pl.ds(pl.multiple_of(units + t * 256, 256), 256)],
                preferred_element_type=F32,
            )
            hid[:, pl.ds(at, 256)] = (gate / (1.0 + jnp.exp(-gate)) * up).astype(BF16)

        if first:
            load_d.wait()

        for h in range(2):
            for t in range(2):
                lo = h * half + t * (half // 2)
                r = jnp.dot(hid[...], wd[:, lo : lo + half // 2], preferred_element_type=F32)
                r = r * weight
                at = slice(t * (half // 2), (t + 1) * (half // 2))
                for k in range(2):
                    own[q, b, h, k, :, at] = r[4 * k * part : (4 * k + 2) * part]
                    csend[q, b, h, k, :, at] = r[(4 * k + 2) * part : (4 * k + 4) * part].astype(
                        BF16
                    )
            core_copy(q, b, h).start()

    def to_x(q, b):
        for h in range(2):
            core_copy(q, b, h).wait_recv()
            total = own[q, b, h, :, part:, :] + crecv[q, b, h, :, part:, :].astype(F32)
            xsend[q, b, h] = total.astype(BF16)
            x_copy(q, b, h).start()

    def to_z(q, b):
        for h in range(2):
            x_copy(q, b, h).wait_recv()
            for k in range(2):
                total = own[q, b, h, k, :part, :] + crecv[q, b, h, k, :part, :].astype(F32)
                total = total + xrecv[q, b, h, k].astype(F32)
                plane = 2 * b + k
                if plane == 0:
                    at = slice(h * half, (h + 1) * half)
                    out_ref[at_rows(q), at] = middle[at_rows(q), at] + total
                else:
                    zsend[q, plane - 1, h] = total.astype(BF16)
                    z_copy(q, plane, h).start()

    def finish(q):
        for k in range(1, 4):
            for h in range(2):
                at = slice(h * half, (h + 1) * half)
                z_copy(q, k, h).wait_recv()
                out_ref[at_rows(q), at] += zrecv[q, k - 1, h].astype(F32)

    expert = lax.broadcasted_iota(jnp.int32, (LANES, rows), 0)
    nums = jnp.zeros((LANES, rows), F32)
    for k in range(ids_ref.shape[0]):
        num = gates_ref[k : k + 1, :].astype(F32)
        nums = nums + jnp.where(expert == ids_ref[k : k + 1, :], num, F32(0))
    nums = nums.T.astype(BF16)
    for q in range(2):
        xall[q, 0, 0, :, width:] = nums[at_rows(q)]
    load_res.wait()

    @pl.when(outer)
    def _():
        for u in range(4):
            att_out(0, u).wait_send()
            w_copy(3 + u).start()
        product_own(0)
        product_own(1)
        for u in range(4):
            att_wait(2, 0, u)
        product_far(2, 0)
        w_copy(3).wait_send()
        w_copy(7).start()
        p_to_x(0, 0)
        p_to_x(0, 1)
        w_copy(4).wait_send()
        att_out(1, 0).start()
        p_to_x(2, 0)
        for u in range(3):
            w_copy(5 + u).wait_send()
            att_out(1, 1 + u).start()
        p_to_z(0, 0)
        p_to_z(0, 1)
        p_to_z(2, 0)
        for u in range(4):
            att_wait(3, 0, u)
        product_far(3, 0)
        p_to_x(3, 0)
        for u in range(4):
            att_wait(2, 1, u)
        product_far(2, 1)
        p_to_z(3, 0)
        p_to_x(2, 1)
        normalise(0, True)
        gather_start(0, False)
        for u in range(4):
            att_wait(3, 1, u)
        product_far(3, 1)
        p_to_z(2, 1)
        p_to_x(3, 1)
        pass_z(0, 1, False)
        pass_x(0, 0)
        p_to_z(3, 1)
        pass_z(0, 2, False)
        normalise(1, True)
        gather_start(1, False)

    @pl.when(inner)
    def _():
        for u in range(4):
            pass_att(3, 2, 0, u, 1)
        for p in range(3):
            pass_w(p)
        for u in range(4):
            pass_att(1, 2, 0, u, 3)
            att_out(1, u).start()
        product_own(0)
        product_own(1)
        product_far(2, 0)
        for u in range(2):
            pass_att(2, 3, 0, u, 1)
        p_to_x(0, 0)
        p_to_x(0, 1)
        p_to_x(2, 0)
        pass_w(3)
        for u in range(2, 4):
            pass_att(2, 3, 0, u, 1)
        pass_w(4)
        product_far(3, 0)
        pass_w(5)
        p_to_z(0, 0)
        p_to_z(0, 1)
        p_to_z(2, 0)
        pass_w(6)
        p_to_x(3, 0)
        pass_w(7)
        for u in range(4):
            pass_att(3, 2, 1, u, 1)
        p_to_z(3, 0)
        pass_att(1, 2, 1, 0, 3)
        for p in range(8):
            w_pass(p).wait_recv()
        product_near(0)
        for u in range(1, 4):
            pass_att(1, 2, 1, u, 3)
        p_to_x(1, 0)
        product_far(2, 1)
        for u in range(2):
            pass_att(2, 3, 1, u, 1)
        p_to_x(2, 1)
        p_to_z(1, 0)
        normalise(0, False)
        gather_start(0, True)
        product_near(1)
        for u in range(2, 4):
            pass_att(2, 3, 1, u, 1)
        p_to_x(1, 1)
        product_far(3, 1)
        p_to_z(2, 1)
        p_to_x(3, 1)
        p_to_z(1, 1)
        pass_z(0, 3, True)
        pass_z(0, 1, True)
        pass_x(0, 0)
        p_to_z(3, 1)
        pass_z(0, 2, True)
        normalise(1, False)
        gather_start(1, True)

    pass_x(0, 1)
    gather_far(0)
    compute(0, 0, True)
    gather_near(1)
    pass_x(0, 2)
    pass_x(0, 3)
    pass_x(1, 0)
    gather_mid(1)
    compute(0, 1)
    gather_far(1)
    to_x(0, 1)
    pass_x(1, 1)
    to_x(0, 0)
    compute(1, 0)
    pass_x(1, 2)
    pass_x(1, 3)
    to_z(0, 1)
    compute(1, 1)
    to_x(1, 1)
    to_x(1, 0)
    to_z(0, 0)
    to_z(1, 1)
    to_z(1, 0)
    finish(0)
    finish(1)

    for q in range(2):
        for n in (0, 2, 3):
            p_core(n, q).wait_send()
            p_x(n, q).wait_send()
            if n > 0:
                p_z(n, q).wait_send()
        z_own(q, False).wait_send()
        for k in range(4):
            x_in(q, k).wait_send()
            for i in range(2):
                core_in(q, k, i).wait_send()
        for b in range(2):
            for h in range(2):
                core_copy(q, b, h).wait_send()
                x_copy(q, b, h).wait_send()
        for k in range(1, 4):
            for h in range(2):
                z_copy(q, k, h).wait_send()

    @pl.when(outer)
    def _():
        for u in range(4):
            att_out(1, u).wait_send()
        for p in range(3):
            w_copy(p).wait_send()

    @pl.when(inner)
    def _():
        for p in range(8):
            w_pass(p).wait_send()
        for q in range(2):
            for u in range(4):
                att_out(q, u).wait_send()
                att_copy(1, 2, q, u, at_plane(3)).wait_send()
                att_copy(3, 2, q, u, at_plane(1)).wait_send()
                att_copy(2, 3, q, u, at_plane(1)).wait_send()
            p_core(1, q).wait_send()
            p_x(1, q).wait_send()
            p_z(1, q).wait_send()
            z_own(q, True).wait_send()
            for k in range(1, 4):
                z_pass(q, k).wait_send()


def grid_shards(
    queries,
    new_keys,
    new_values,
    cache_keys,
    cache_values,
    cache_len,
    out_weight,
    residual,
    norm_gain,
    expert_ids,
    gate_nums,
    w_gate_up,
    w_down,
):
    rows, width = residual.shape
    units = w_down.shape[1]
    cols = out_weight.shape[1]
    heads = queries.shape[2]
    part = rows // 2
    half = width // 2
    vmem = pl.BlockSpec(memory_space=pltpu.VMEM)
    hbm = pl.BlockSpec(memory_space=pl.ANY)
    dma = pltpu.SemaphoreType.DMA
    return pl.pallas_call(
        layer_kernel,
        out_shape=jax.ShapeDtypeStruct((rows, width), F32),
        in_specs=[pl.BlockSpec(memory_space=pltpu.SMEM)] + [hbm] * 9 + [vmem] * 3,
        out_specs=vmem,
        scratch_shapes=[
            pltpu.VMEM(queries.shape, BF16),
            pltpu.VMEM(new_keys.shape, BF16),
            pltpu.VMEM(new_values.shape, BF16),
            pltpu.VMEM(cache_keys.shape, BF16),
            pltpu.VMEM(cache_values.shape, BF16),
            pltpu.VMEM(out_weight.shape, BF16),
            pltpu.VMEM(out_weight.shape, BF16),
            dma((6,)),
            pltpu.VMEM((4, 2, 4, part, heads), BF16),
            pltpu.VMEM((2, 5, 2 * part, cols), F32),
            pltpu.VMEM((2, 5, 2 * part, cols), F32),
            pltpu.VMEM((2, 5, 2 * part, cols), F32),
            pltpu.VMEM((2, 5, part, cols), BF16),
            pltpu.VMEM((2, 5, part, cols), BF16),
            pltpu.VMEM((2, 3, part, cols), BF16),
            pltpu.VMEM((2, 3, part, cols), BF16),
            dma((32,)),
            dma((32,)),
            dma((16,)),
            dma((16,)),
            dma((16,)),
            dma((16,)),
            dma((6,)),
            dma((6,)),
            pltpu.VMEM((width, 2 * units), BF16),
            pltpu.VMEM((units, width), BF16),
            pltpu.VMEM((rows, width), F32),
            dma((3,)),
            pltpu.VMEM((2, 4, 4, part, width + LANES), BF16),
            pltpu.VMEM((8 * part, units), BF16),
            pltpu.VMEM((2, 2, 2, 2, 2 * part, half), F32),
            pltpu.VMEM((2, 2, 2, 2, 2 * part, half), BF16),
            pltpu.VMEM((2, 2, 2, 2, 2 * part, half), BF16),
            pltpu.VMEM((2, 2, 2, 2, part, half), BF16),
            pltpu.VMEM((2, 2, 2, 2, part, half), BF16),
            pltpu.VMEM((2, 3, 2, part, half), BF16),
            pltpu.VMEM((2, 3, 2, part, half), BF16),
            dma((34,)),
            dma((32,)),
            dma((8,)),
            dma((8,)),
            dma((8,)),
            dma((8,)),
            dma((12,)),
            dma((12,)),
        ],
        compiler_params=pltpu.CompilerParams(
            collective_id=0, has_side_effects=True, vmem_limit_bytes=58 << 20
        ),
    )(
        cache_len, queries, new_keys, new_values, cache_keys, cache_values, out_weight,
        residual, w_gate_up, w_down, norm_gain.reshape(1, width), expert_ids.T, gate_nums.T,
    )


def attend_session(packed):
    q_s, k_new, v_new, k_old, v_old, length = packed
    n_new = q_s.shape[0]
    n_old = k_old.shape[0]
    kv_count = k_old.shape[-1] // HD
    group_size = q_s.shape[-1] // (kv_count * HD)
    q_four = q_s.reshape(n_new, kv_count, group_size, HD)
    k_old3 = k_old.reshape(n_old, kv_count, HD)
    v_old3 = v_old.reshape(n_old, kv_count, HD)
    k_new3 = k_new.reshape(n_new, kv_count, HD)
    v_new3 = v_new.reshape(n_new, kv_count, HD)
    scale = 1.0 / HD**0.5
    s_old = jnp.einsum("ikgd,jkd->kgij", q_four, k_old3, preferred_element_type=jnp.float32) * scale
    s_new = jnp.einsum("ikgd,jkd->kgij", q_four, k_new3, preferred_element_type=jnp.float32) * scale
    valid_old = jnp.arange(n_old, dtype=jnp.int32) < length
    s_old = jnp.where(valid_old[None, None, None, :], s_old, jnp.float32(-1e30))
    causal = (
        jnp.arange(n_new, dtype=jnp.int32)[None, :] <= jnp.arange(n_new, dtype=jnp.int32)[:, None]
    )
    s_new = jnp.where(causal[None, None], s_new, jnp.float32(-1e30))
    top = jnp.maximum(jnp.max(s_old, -1, keepdims=True), jnp.max(s_new, -1, keepdims=True))
    e_old = jnp.exp(s_old - top)
    e_new = jnp.exp(s_new - top)
    total = jnp.sum(e_old, -1, keepdims=True) + jnp.sum(e_new, -1, keepdims=True)
    p_old = (e_old / total).astype(jnp.bfloat16)
    p_new = (e_new / total).astype(jnp.bfloat16)
    out = jnp.einsum("kgij,jkd->ikgd", p_old, v_old3, preferred_element_type=jnp.float32)
    out = out + jnp.einsum("kgij,jkd->ikgd", p_new, v_new3, preferred_element_type=jnp.float32)
    return out.reshape(n_new, kv_count * group_size * HD).astype(jnp.bfloat16)


def shards(
    queries,
    new_keys,
    new_values,
    cache_keys,
    cache_values,
    cache_len,
    out_weight,
    residual,
    norm_gain,
    expert_ids,
    gate_nums,
    w_gate_up,
    w_down,
):
    attended = lax.map(
        attend_session, (queries, new_keys, new_values, cache_keys, cache_values, cache_len)
    )
    local_rows = attended.reshape(attended.shape[0] * attended.shape[1], attended.shape[2])
    spread = jnp.dot(
        lax.all_gather(local_rows, "exp", axis=0, tiled=True),
        out_weight,
        preferred_element_type=jnp.float32,
    )
    partial_value = lax.all_to_all(spread, "exp", split_axis=0, concat_axis=1, tiled=True)
    projected = lax.psum_scatter(partial_value, "attn", scatter_dimension=0, tiled=True)
    middle = residual + projected
    meansq = jnp.mean(middle * middle, -1, keepdims=True)
    normed = (middle * lax.rsqrt(meansq + 1e-06) * norm_gain).astype(jnp.bfloat16)
    tok_rows = expert_ids.shape[0]
    top_count = expert_ids.shape[1]
    exp_dev = w_gate_up.shape[0]
    hidden_units = w_down.shape[1]
    n_experts = exp_dev * lax.axis_size("attn") * lax.axis_size("exp")
    capacity = max(2, 2 * tok_rows * top_count // n_experts)
    flat_ids = expert_ids.reshape(-1)
    order = jnp.arange(flat_ids.shape[0], dtype=jnp.int32)
    earlier = (flat_ids[:, None] == flat_ids[None, :]) & (order[None, :] < order[:, None])
    slot = jnp.sum(earlier.astype(jnp.int32), -1)
    target = (flat_ids * capacity + slot).reshape(tok_rows, top_count)
    places = jnp.arange(n_experts * capacity, dtype=jnp.int32)
    placing = jnp.sum((places[:, None, None] == target[None, :, :]).astype(jnp.int32), -1).astype(
        jnp.bfloat16
    )
    sent = jnp.dot(placing, normed, preferred_element_type=jnp.float32).astype(jnp.bfloat16)
    sent = sent.reshape(n_experts, capacity, normed.shape[1])
    block = lax.all_to_all(sent, ("attn", "exp"), split_axis=0, concat_axis=0, tiled=True)
    n_src = block.shape[0] // exp_dev
    rows_four = block.reshape(n_src, exp_dev, block.shape[1], block.shape[2])
    both = jnp.einsum("sjmd,jdf->sjmf", rows_four, w_gate_up, preferred_element_type=jnp.float32)
    hidden = (jax.nn.silu(both[..., :hidden_units]) * both[..., hidden_units:]).astype(jnp.bfloat16)
    result = jnp.einsum("sjmf,jfd->sjmd", hidden, w_down, preferred_element_type=jnp.float32)
    result = result.astype(jnp.bfloat16).reshape(block.shape)
    returned = lax.all_to_all(result, ("attn", "exp"), split_axis=0, concat_axis=0, tiled=True)
    picked = (
        returned[flat_ids, slot].reshape(tok_rows, top_count, normed.shape[1]).astype(jnp.float32)
    )
    numer = gate_nums.astype(jnp.float32)
    weights = numer / jnp.sum(numer, -1, keepdims=True)
    return middle + jnp.sum(picked * weights[:, :, None], 1)


def fits_grid(mesh):
    return mesh.shape["groups"] == 2 and mesh.shape["attn"] == 4 and mesh.shape["exp"] == 4


def solution(mesh):
    in_specs = (
        P(("groups", "exp"), None, "attn"),
        P(("groups", "exp"), None, "attn"),
        P(("groups", "exp"), None, "attn"),
        P(("groups", "exp"), None, "attn"),
        P(("groups", "exp"), None, "attn"),
        P(("groups", "exp")),
        P("attn", "exp"),
        P(("groups", "exp", "attn"), None),
        P(),
        P(("groups", "exp", "attn"), None),
        P(("groups", "exp", "attn"), None),
        P(("attn", "exp"), None, None),
        P(("attn", "exp"), None, None),
    )
    out_specs = P(("groups", "exp", "attn"), None)
    body = grid_shards if fits_grid(mesh) else shards
    return jax.shard_map(body, mesh=mesh, in_specs=in_specs, out_specs=out_specs, check_vma=False)
```

```python
import jax
import jax.numpy as jnp
from jax import lax
from jax.experimental import pallas as pl
from jax.experimental.pallas import tpu as pltpu
from jax.sharding import PartitionSpec as P

HD = 128
LANES = 128
F32 = jnp.float32
BF16 = jnp.bfloat16


def places():
    g = lax.axis_index("groups")
    a = lax.axis_index("attn")
    z = lax.axis_index("exp")
    core = a + 1 - 2 * (a % 2)
    across = (a + 2) % 4
    planes = [z, z + 1 - 2 * (z % 2), (z + 2) % 4, 3 - z]
    inner = (z == 1) | (z == 2)
    return g, a, z, core, across, planes, inner


def meet(g, a, z, core, across, planes):
    barrier = pltpu.get_barrier_semaphore()
    peers = [(g, core, z), (g, across, z), (1 - g, a, z)] + [(g, a, p) for p in planes[1:]]
    for peer in peers:
        pl.semaphore_signal(barrier, inc=1, device_id=peer, device_id_type=pl.DeviceIdType.MESH)
    pl.semaphore_wait(barrier, len(peers))


def copy_to(src, dst, sems, i, j, where):
    return pltpu.make_async_remote_copy(
        src_ref=src,
        dst_ref=dst,
        send_sem=sems[0].at[i],
        recv_sem=sems[1].at[j],
        device_id=where,
        device_id_type=pl.DeviceIdType.MESH,
    )


def attend(q, k_new, v_new, k_old, v_old, length):
    n_new, n_old = q.shape[0], k_old.shape[0]
    kv_count = k_old.shape[1] // HD
    group = q.shape[1] // (kv_count * HD)
    scale = 1.0 / HD**0.5
    dims = (((1,), (1,)), ((), ()))
    heads = []
    for j in range(kv_count):
        cols = slice(j * HD, (j + 1) * HD)
        rows = jnp.concatenate(
            [q[:, (j * group + g) * HD : (j * group + g + 1) * HD] for g in range(group)], 0
        )
        s_old = lax.dot_general(rows, k_old[:, cols], dims, preferred_element_type=F32) * scale
        s_new = lax.dot_general(rows, k_new[:, cols], dims, preferred_element_type=F32) * scale
        valid = lax.broadcasted_iota(jnp.int32, s_old.shape, 1) < length
        s_old = jnp.where(valid, s_old, F32(-1e30))
        token = lax.broadcasted_iota(jnp.int32, (group, n_new, n_new), 1).reshape(s_new.shape)
        causal = lax.broadcasted_iota(jnp.int32, s_new.shape, 1) <= token
        s_new = jnp.where(causal, s_new, F32(-1e30))
        top = jnp.maximum(jnp.max(s_old, -1, keepdims=True), jnp.max(s_new, -1, keepdims=True))
        e_old = jnp.exp(s_old - top)
        e_new = jnp.exp(s_new - top)
        inv = 1.0 / (jnp.sum(e_old, -1, keepdims=True) + jnp.sum(e_new, -1, keepdims=True))
        p_old = (e_old * inv).astype(BF16)
        p_new = (e_new * inv).astype(BF16)
        out = jnp.dot(p_old, v_old[:, cols], preferred_element_type=F32)
        out = out + jnp.dot(p_new, v_new[:, cols], preferred_element_type=F32)
        out = out.astype(BF16)
        heads += [out[g * n_new : (g + 1) * n_new] for g in range(group)]
    return jnp.concatenate(heads, 1)


def layer_kernel(
    len_ref, q_hbm, kn_hbm, vn_hbm, kc_hbm, vc_hbm, wo_hbm, res_hbm, wgu_hbm, wd_hbm,
    gain_ref, ids_ref, gates_ref, out_ref,
    q_ref, kn_ref, vn_ref, kc_ref, vc_ref, wo_ref, wo_near, lsem, att,
    p_own, p_csend, p_crecv, p_xsend, p_xrecv, p_zsend, p_zrecv,
    a_s, a_r, w_s, w_r, p_s, p_r, pz_s, pz_r,
    wgu, wd, middle, wsem, xall, hid,
    own, csend, crecv, xsend, xrecv, zsend, zrecv,
    g_s, g_r, c_s, c_r, x_s, x_r, z_s, z_r,
):
    g, a, z, core, across, planes, inner = places()
    outer = jnp.logical_not(inner)
    opposite = (core + 2) % 4
    rows, width = out_ref.shape
    part = rows // 2
    cols = wo_ref.shape[1]
    heads = wo_ref.shape[0]
    units = wd.shape[0]
    mine = a * 4 + z
    half = width // 2
    w_rows = heads // 16

    at_core = (g, core, z)
    at_across = (g, across, z)
    at_group = (1 - g, a, z)

    def at_plane(k):
        return (g, a, planes[k])

    inner_int = inner.astype(jnp.int32)
    first_far = 2 + inner_int
    second_far = 3 - inner_int
    at_first = (g, a, planes[2] + inner_int * (planes[3] - planes[2]))
    at_second = (g, a, planes[3] + inner_int * (planes[2] - planes[3]))
    at_out = (g, a, planes[1] + inner_int * (planes[3] - planes[1]))
    out_slot = 1 + 2 * inner_int
    w_at = [
        pl.ds(pl.multiple_of(g * (heads // 2) + p * w_rows, w_rows), w_rows) for p in range(8)
    ]

    loads = [
        pltpu.make_async_copy(src, dst, lsem.at[i])
        for i, (src, dst) in enumerate(
            [
                (wo_hbm, wo_ref),
                (q_hbm, q_ref),
                (kn_hbm, kn_ref),
                (vn_hbm, vn_ref),
                (kc_hbm, kc_ref),
                (vc_hbm, vc_ref),
            ]
        )
    ]
    load_res = pltpu.make_async_copy(res_hbm, middle, wsem.at[2])
    load_gu = pltpu.make_async_copy(wgu_hbm.at[0], wgu, wsem.at[0])
    load_d = pltpu.make_async_copy(wd_hbm.at[0], wd, wsem.at[1])
    for load in loads + [load_res, load_gu, load_d]:
        load.start()
    meet(g, a, z, core, across, planes)

    def att_copy(k_from, k_to, q, u, where):
        return copy_to(
            att.at[k_from, q, u], att.at[k_to, q, u],
            (a_s, a_r), k_from * 8 + 4 * q + u, k_to * 8 + 4 * q + u, where,
        )

    def att_out(q, u):
        return att_copy(0, out_slot, q, u, at_out)

    def att_wait(k, q, u):
        att_copy(0, k, q, u, at_plane(1)).wait_recv()

    def w_copy(p):
        return copy_to(wo_ref.at[w_at[p]], wo_near.at[w_at[p]], (w_s, w_r), p, p, at_plane(1))

    def w_pass(p):
        return copy_to(
            wo_near.at[w_at[p]], wo_near.at[w_at[p]], (w_s, w_r), 8 + p, 8 + p, at_group
        )

    loads[0].wait()

    @pl.when(outer)
    def _():
        for p in range(3):
            w_copy(p).start()

    for load in loads[1:]:
        load.wait()

    @pl.loop(0, 8)
    def _(j):
        q = j // 4
        u = j % 4
        t = 2 * u + q
        att[0, q, u] = attend(q_ref[t], kn_ref[t], vn_ref[t], kc_ref[t], vc_ref[t], len_ref[t])

        @pl.when(j < 4)
        def _():
            att_out(q, u).start()

    groups = [(0, 1), (1, 3), (3, 4), (4, 5)]

    def p_core(n, q):
        lo, hi = groups[n]
        i = 4 * q + n
        return copy_to(p_csend.at[q, lo:hi], p_crecv.at[q, lo:hi], (p_s, p_r), i, i, at_core)

    def p_x(n, q):
        lo, hi = groups[n]
        i = 8 + 4 * q + n
        return copy_to(p_xsend.at[q, lo:hi], p_xrecv.at[q, lo:hi], (p_s, p_r), i, i, at_across)

    def p_z(n, q):
        k, where = {1: (1, at_plane(1)), 2: (first_far, at_first), 3: (second_far, at_second)}[n]
        return copy_to(
            p_zsend.at[q, n - 1], p_zrecv.at[q, k - 1], (pz_s, pz_r),
            3 * q + n - 1, 3 * q + k - 1, where,
        )

    def att_rows(k, q):
        return jnp.concatenate(
            [att[k, q, a], att[k, q, across], att[k, q, core], att[k, q, opposite]], 0
        )

    def keep(job, q, r):
        p_own[q, job] = r[: 2 * part]
        p_csend[q, job] = r[2 * part :]

    def product_own(q):
        keep(0, q, jnp.dot(att_rows(0, q), wo_ref[...], preferred_element_type=F32))
        p_core(0, q).start()

    def product_near(q):
        keep(1, q, jnp.dot(att_rows(1, q), wo_ref[...], preferred_element_type=F32))
        keep(2, q, jnp.dot(att_rows(0, q), wo_near[...], preferred_element_type=F32))
        p_core(1, q).start()

    def product_far(n, q):
        k = first_far if n == 2 else second_far
        keep(n + 1, q, jnp.dot(att_rows(k, q), wo_ref[...], preferred_element_type=F32))
        p_core(n, q).start()

    def p_to_x(n, q):
        lo, hi = groups[n]
        p_core(n, q).wait_recv()
        for job in range(lo, hi):
            p_xsend[q, job] = (p_own[q, job, part:] + p_crecv[q, job, part:]).astype(BF16)
        p_x(n, q).start()

    def at_cols(k):
        return pl.ds(pl.multiple_of(planes[k] * cols, LANES), cols)

    def at_rows(q):
        return slice(q * part, (q + 1) * part)

    def p_total(job, q):
        return p_own[q, job, :part] + p_crecv[q, job, :part] + p_xrecv[q, job].astype(F32)

    def p_to_z(n, q):
        p_x(n, q).wait_recv()
        if n == 0:
            middle[at_rows(q), at_cols(0)] += p_total(0, q)
        if n == 1:
            middle[at_rows(q), at_cols(1)] += p_total(2, q)
        if n > 0:
            p_zsend[q, n - 1] = p_total({1: 1, 2: 3, 3: 4}[n], q).astype(BF16)
            p_z(n, q).start()

    def p_take(k, q):
        copy_to(
            p_zsend.at[q, k - 1], p_zrecv.at[q, k - 1], (pz_s, pz_r),
            3 * q + k - 1, 3 * q + k - 1, at_plane(k),
        ).wait_recv()
        middle[at_rows(q), at_cols(k)] += p_zrecv[q, k - 1].astype(F32)

    def normalise(q, near):
        if near:
            p_take(1, q)
        p_take(2, q)
        p_take(3, q)
        m = middle[at_rows(q), :]
        meansq = jnp.mean(m * m, -1, keepdims=True)
        normed = (m * lax.rsqrt(meansq + 1e-06) * gain_ref[...]).astype(BF16)
        xall[q, 0, 0, :, :width] = normed

    def pass_att(k_from, k_to, q, u, plane):
        att_wait(k_from, q, u)
        att_copy(k_from, k_to, q, u, at_plane(plane)).start()

    def pass_w(p):
        w_copy(p).wait_recv()
        w_pass(p).start()

    def rows_copy(q, s, ks, i_from, kd, i_to, where):
        return copy_to(
            xall.at[q, ks, i_from], xall.at[q, kd, i_to], (g_s, g_r),
            17 * q + s, 16 * q + 4 * kd + i_to, where,
        )

    def z_own(q, far):
        if far:
            return rows_copy(q, 1, 0, 0, 3, 0, at_plane(3))
        return rows_copy(q, 0, 0, 0, 1, 0, at_plane(1))

    def z_pass(q, k):
        kd = {1: 2, 3: 2, 2: 3}[k]
        return rows_copy(q, {1: 2, 3: 3, 2: 4}[k], k, 0, kd, 0, at_plane(3 if k == 1 else 1))

    def x_in(q, k):
        return rows_copy(q, 5 + k, k, 0, k, 1, at_across)

    def core_in(q, k, i):
        return rows_copy(q, 9 + 2 * k + i, k, i, k, 2 + i, at_core)

    def gather_start(q, far):
        if far:
            z_own(q, True).start()
        x_in(q, 0).start()
        z_own(q, False).start()
        core_in(q, 0, 0).start()

    def arrived(q, k, i):
        rows_copy(q, 0, 0, 0, k, i, at_plane(1)).wait_recv()

    def pass_z(q, k, on):
        arrived(q, k, 0)
        if on:
            z_pass(q, k).start()
        x_in(q, k).start()
        core_in(q, k, 0).start()

    def pass_x(q, k):
        arrived(q, k, 1)
        core_in(q, k, 1).start()

    def gather_near(q):
        @pl.when(inner)
        def _():
            pass_z(q, 3, True)
            pass_z(q, 1, True)

        @pl.when(outer)
        def _():
            pass_z(q, 1, False)

    def gather_mid(q):
        @pl.when(inner)
        def _():
            pass_z(q, 2, True)

        @pl.when(outer)
        def _():
            pass_z(q, 2, False)

    def gather_far(q):
        @pl.when(outer)
        def _():
            pass_z(q, 3, False)

    def core_copy(q, b, h):
        i = 4 * q + 2 * b + h
        return copy_to(csend.at[q, b, h], crecv.at[q, b, h], (c_s, c_r), i, i, at_core)

    def x_copy(q, b, h):
        i = 4 * q + 2 * b + h
        return copy_to(xsend.at[q, b, h], xrecv.at[q, b, h], (x_s, x_r), i, i, at_across)

    def z_copy(q, k, h):
        i = 6 * q + 2 * (k - 1) + h
        return copy_to(zsend.at[q, k - 1, h], zrecv.at[q, k - 1, h], (z_s, z_r), i, i, at_plane(k))

    def compute(q, b, first=False):
        for k in (2 * b, 2 * b + 1):
            for i in (2, 3):
                arrived(q, k, i)
        if first:
            load_gu.wait()
        block = xall[q, 2 * b : 2 * b + 2].reshape(8 * part, width + LANES)
        x = block[:, :width]
        nums = block[:, width:].astype(F32)
        lane = lax.broadcasted_iota(jnp.int32, nums.shape, 1)
        num = jnp.sum(jnp.where(lane == mine, nums, F32(0)), -1, keepdims=True)
        weight = num / jnp.sum(nums, -1, keepdims=True)

        @pl.loop(0, units // 256, unroll=True)
        def _(t):
            at = pl.multiple_of(t * 256, 256)
            gate = jnp.dot(x, wgu[:, pl.ds(at, 256)], preferred_element_type=F32)
            up = jnp.dot(
                x,
                wgu[:, pl.ds(pl.multiple_of(units + t * 256, 256), 256)],
                preferred_element_type=F32,
            )
            hid[:, pl.ds(at, 256)] = (gate / (1.0 + jnp.exp(-gate)) * up).astype(BF16)

        if first:
            load_d.wait()

        for h in range(2):
            for t in range(2):
                lo = h * half + t * (half // 2)
                r = jnp.dot(hid[...], wd[:, lo : lo + half // 2], preferred_element_type=F32)
                r = r * weight
                at = slice(t * (half // 2), (t + 1) * (half // 2))
                for k in range(2):
                    own[q, b, h, k, :, at] = r[4 * k * part : (4 * k + 2) * part]
                    csend[q, b, h, k, :, at] = r[(4 * k + 2) * part : (4 * k + 4) * part].astype(
                        BF16
                    )
            core_copy(q, b, h).start()

    def to_x(q, b):
        for h in range(2):
            core_copy(q, b, h).wait_recv()
            total = own[q, b, h, :, part:, :] + crecv[q, b, h, :, part:, :].astype(F32)
            xsend[q, b, h] = total.astype(BF16)
            x_copy(q, b, h).start()

    def to_z(q, b):
        for h in range(2):
            x_copy(q, b, h).wait_recv()
            for k in range(2):
                total = own[q, b, h, k, :part, :] + crecv[q, b, h, k, :part, :].astype(F32)
                total = total + xrecv[q, b, h, k].astype(F32)
                plane = 2 * b + k
                if plane == 0:
                    at = slice(h * half, (h + 1) * half)
                    out_ref[at_rows(q), at] = middle[at_rows(q), at] + total
                else:
                    zsend[q, plane - 1, h] = total.astype(BF16)
                    z_copy(q, plane, h).start()

    def finish(q):
        for k in range(1, 4):
            for h in range(2):
                at = slice(h * half, (h + 1) * half)
                z_copy(q, k, h).wait_recv()
                out_ref[at_rows(q), at] += zrecv[q, k - 1, h].astype(F32)

    expert = lax.broadcasted_iota(jnp.int32, (LANES, rows), 0)
    nums = jnp.zeros((LANES, rows), F32)
    for k in range(ids_ref.shape[0]):
        num = gates_ref[k : k + 1, :].astype(F32)
        nums = nums + jnp.where(expert == ids_ref[k : k + 1, :], num, F32(0))
    nums = nums.T.astype(BF16)
    for q in range(2):
        xall[q, 0, 0, :, width:] = nums[at_rows(q)]
    load_res.wait()

    @pl.when(outer)
    def _():
        for u in range(4):
            att_out(0, u).wait_send()
            w_copy(3 + u).start()
        product_own(0)
        product_own(1)
        for u in range(4):
            att_wait(2, 0, u)
        product_far(2, 0)
        w_copy(3).wait_send()
        w_copy(7).start()
        p_to_x(0, 0)
        p_to_x(0, 1)
        w_copy(4).wait_send()
        att_out(1, 0).start()
        p_to_x(2, 0)
        for u in range(3):
            w_copy(5 + u).wait_send()
            att_out(1, 1 + u).start()
        p_to_z(0, 0)
        p_to_z(0, 1)
        p_to_z(2, 0)
        for u in range(4):
            att_wait(3, 0, u)
        product_far(3, 0)
        p_to_x(3, 0)
        for u in range(4):
            att_wait(2, 1, u)
        product_far(2, 1)
        p_to_z(3, 0)
        p_to_x(2, 1)
        normalise(0, True)
        gather_start(0, False)
        for u in range(4):
            att_wait(3, 1, u)
        product_far(3, 1)
        p_to_z(2, 1)
        p_to_x(3, 1)
        pass_z(0, 1, False)
        pass_x(0, 0)
        p_to_z(3, 1)
        pass_z(0, 2, False)
        normalise(1, True)
        gather_start(1, False)

    @pl.when(inner)
    def _():
        for u in range(4):
            pass_att(3, 2, 0, u, 1)
        for p in range(3):
            pass_w(p)
        for u in range(4):
            pass_att(1, 2, 0, u, 3)
            att_out(1, u).start()
        product_own(0)
        product_own(1)
        product_far(2, 0)
        for u in range(2):
            pass_att(2, 3, 0, u, 1)
        p_to_x(0, 0)
        p_to_x(0, 1)
        p_to_x(2, 0)
        pass_w(3)
        for u in range(2, 4):
            pass_att(2, 3, 0, u, 1)
        pass_w(4)
        product_far(3, 0)
        pass_w(5)
        p_to_z(0, 0)
        p_to_z(0, 1)
        p_to_z(2, 0)
        pass_w(6)
        p_to_x(3, 0)
        pass_w(7)
        for u in range(4):
            pass_att(3, 2, 1, u, 1)
        p_to_z(3, 0)
        pass_att(1, 2, 1, 0, 3)
        for p in range(8):
            w_pass(p).wait_recv()
        product_near(0)
        for u in range(1, 4):
            pass_att(1, 2, 1, u, 3)
        p_to_x(1, 0)
        product_far(2, 1)
        for u in range(2):
            pass_att(2, 3, 1, u, 1)
        p_to_x(2, 1)
        p_to_z(1, 0)
        normalise(0, False)
        gather_start(0, True)
        product_near(1)
        for u in range(2, 4):
            pass_att(2, 3, 1, u, 1)
        p_to_x(1, 1)
        product_far(3, 1)
        p_to_z(2, 1)
        p_to_x(3, 1)
        p_to_z(1, 1)
        pass_z(0, 3, True)
        pass_z(0, 1, True)
        pass_x(0, 0)
        p_to_z(3, 1)
        pass_z(0, 2, True)
        normalise(1, False)
        gather_start(1, True)

    pass_x(0, 1)
    gather_far(0)
    compute(0, 0, True)
    gather_near(1)
    pass_x(0, 2)
    pass_x(0, 3)
    pass_x(1, 0)
    gather_mid(1)
    compute(0, 1)
    gather_far(1)
    to_x(0, 1)
    pass_x(1, 1)
    to_x(0, 0)
    compute(1, 0)
    pass_x(1, 2)
    pass_x(1, 3)
    to_z(0, 1)
    compute(1, 1)
    to_x(1, 1)
    to_x(1, 0)
    to_z(0, 0)
    to_z(1, 1)
    to_z(1, 0)
    finish(0)
    finish(1)

    for q in range(2):
        for n in (0, 2, 3):
            p_core(n, q).wait_send()
            p_x(n, q).wait_send()
            if n > 0:
                p_z(n, q).wait_send()
        z_own(q, False).wait_send()
        for k in range(4):
            x_in(q, k).wait_send()
            for i in range(2):
                core_in(q, k, i).wait_send()
        for b in range(2):
            for h in range(2):
                core_copy(q, b, h).wait_send()
                x_copy(q, b, h).wait_send()
        for k in range(1, 4):
            for h in range(2):
                z_copy(q, k, h).wait_send()

    @pl.when(outer)
    def _():
        for u in range(4):
            att_out(1, u).wait_send()
        for p in range(3):
            w_copy(p).wait_send()

    @pl.when(inner)
    def _():
        for p in range(8):
            w_pass(p).wait_send()
        for q in range(2):
            for u in range(4):
                att_out(q, u).wait_send()
                att_copy(1, 2, q, u, at_plane(3)).wait_send()
                att_copy(3, 2, q, u, at_plane(1)).wait_send()
                att_copy(2, 3, q, u, at_plane(1)).wait_send()
            p_core(1, q).wait_send()
            p_x(1, q).wait_send()
            p_z(1, q).wait_send()
            z_own(q, True).wait_send()
            for k in range(1, 4):
                z_pass(q, k).wait_send()


def grid_shards(
    queries,
    new_keys,
    new_values,
    cache_keys,
    cache_values,
    cache_len,
    out_weight,
    residual,
    norm_gain,
    expert_ids,
    gate_nums,
    w_gate_up,
    w_down,
):
    rows, width = residual.shape
    units = w_down.shape[1]
    cols = out_weight.shape[1]
    heads = queries.shape[2]
    part = rows // 2
    half = width // 2
    vmem = pl.BlockSpec(memory_space=pltpu.VMEM)
    hbm = pl.BlockSpec(memory_space=pl.ANY)
    dma = pltpu.SemaphoreType.DMA
    return pl.pallas_call(
        layer_kernel,
        out_shape=jax.ShapeDtypeStruct((rows, width), F32),
        in_specs=[pl.BlockSpec(memory_space=pltpu.SMEM)] + [hbm] * 9 + [vmem] * 3,
        out_specs=vmem,
        scratch_shapes=[
            pltpu.VMEM(queries.shape, BF16),
            pltpu.VMEM(new_keys.shape, BF16),
            pltpu.VMEM(new_values.shape, BF16),
            pltpu.VMEM(cache_keys.shape, BF16),
            pltpu.VMEM(cache_values.shape, BF16),
            pltpu.VMEM(out_weight.shape, BF16),
            pltpu.VMEM(out_weight.shape, BF16),
            dma((6,)),
            pltpu.VMEM((4, 2, 4, part, heads), BF16),
            pltpu.VMEM((2, 5, 2 * part, cols), F32),
            pltpu.VMEM((2, 5, 2 * part, cols), F32),
            pltpu.VMEM((2, 5, 2 * part, cols), F32),
            pltpu.VMEM((2, 5, part, cols), BF16),
            pltpu.VMEM((2, 5, part, cols), BF16),
            pltpu.VMEM((2, 3, part, cols), BF16),
            pltpu.VMEM((2, 3, part, cols), BF16),
            dma((32,)),
            dma((32,)),
            dma((16,)),
            dma((16,)),
            dma((16,)),
            dma((16,)),
            dma((6,)),
            dma((6,)),
            pltpu.VMEM((width, 2 * units), BF16),
            pltpu.VMEM((units, width), BF16),
            pltpu.VMEM((rows, width), F32),
            dma((3,)),
            pltpu.VMEM((2, 4, 4, part, width + LANES), BF16),
            pltpu.VMEM((8 * part, units), BF16),
            pltpu.VMEM((2, 2, 2, 2, 2 * part, half), F32),
            pltpu.VMEM((2, 2, 2, 2, 2 * part, half), BF16),
            pltpu.VMEM((2, 2, 2, 2, 2 * part, half), BF16),
            pltpu.VMEM((2, 2, 2, 2, part, half), BF16),
            pltpu.VMEM((2, 2, 2, 2, part, half), BF16),
            pltpu.VMEM((2, 3, 2, part, half), BF16),
            pltpu.VMEM((2, 3, 2, part, half), BF16),
            dma((34,)),
            dma((32,)),
            dma((8,)),
            dma((8,)),
            dma((8,)),
            dma((8,)),
            dma((12,)),
            dma((12,)),
        ],
        compiler_params=pltpu.CompilerParams(
            collective_id=0, has_side_effects=True, vmem_limit_bytes=58 << 20
        ),
    )(
        cache_len, queries, new_keys, new_values, cache_keys, cache_values, out_weight,
        residual, w_gate_up, w_down, norm_gain.reshape(1, width), expert_ids.T, gate_nums.T,
    )


def attend_session(packed):
    q_s, k_new, v_new, k_old, v_old, length = packed
    n_new = q_s.shape[0]
    n_old = k_old.shape[0]
    kv_count = k_old.shape[-1] // HD
    group_size = q_s.shape[-1] // (kv_count * HD)
    q_four = q_s.reshape(n_new, kv_count, group_size, HD)
    k_old3 = k_old.reshape(n_old, kv_count, HD)
    v_old3 = v_old.reshape(n_old, kv_count, HD)
    k_new3 = k_new.reshape(n_new, kv_count, HD)
    v_new3 = v_new.reshape(n_new, kv_count, HD)
    scale = 1.0 / HD**0.5
    s_old = jnp.einsum("ikgd,jkd->kgij", q_four, k_old3, preferred_element_type=jnp.float32) * scale
    s_new = jnp.einsum("ikgd,jkd->kgij", q_four, k_new3, preferred_element_type=jnp.float32) * scale
    valid_old = jnp.arange(n_old, dtype=jnp.int32) < length
    s_old = jnp.where(valid_old[None, None, None, :], s_old, jnp.float32(-1e30))
    causal = (
        jnp.arange(n_new, dtype=jnp.int32)[None, :] <= jnp.arange(n_new, dtype=jnp.int32)[:, None]
    )
    s_new = jnp.where(causal[None, None], s_new, jnp.float32(-1e30))
    top = jnp.maximum(jnp.max(s_old, -1, keepdims=True), jnp.max(s_new, -1, keepdims=True))
    e_old = jnp.exp(s_old - top)
    e_new = jnp.exp(s_new - top)
    total = jnp.sum(e_old, -1, keepdims=True) + jnp.sum(e_new, -1, keepdims=True)
    p_old = (e_old / total).astype(jnp.bfloat16)
    p_new = (e_new / total).astype(jnp.bfloat16)
    out = jnp.einsum("kgij,jkd->ikgd", p_old, v_old3, preferred_element_type=jnp.float32)
    out = out + jnp.einsum("kgij,jkd->ikgd", p_new, v_new3, preferred_element_type=jnp.float32)
    return out.reshape(n_new, kv_count * group_size * HD).astype(jnp.bfloat16)


def shards(
    queries,
    new_keys,
    new_values,
    cache_keys,
    cache_values,
    cache_len,
    out_weight,
    residual,
    norm_gain,
    expert_ids,
    gate_nums,
    w_gate_up,
    w_down,
):
    attended = lax.map(
        attend_session, (queries, new_keys, new_values, cache_keys, cache_values, cache_len)
    )
    local_rows = attended.reshape(attended.shape[0] * attended.shape[1], attended.shape[2])
    spread = jnp.dot(
        lax.all_gather(local_rows, "exp", axis=0, tiled=True),
        out_weight,
        preferred_element_type=jnp.float32,
    )
    partial_value = lax.all_to_all(spread, "exp", split_axis=0, concat_axis=1, tiled=True)
    projected = lax.psum_scatter(partial_value, "attn", scatter_dimension=0, tiled=True)
    middle = residual + projected
    meansq = jnp.mean(middle * middle, -1, keepdims=True)
    normed = (middle * lax.rsqrt(meansq + 1e-06) * norm_gain).astype(jnp.bfloat16)
    tok_rows = expert_ids.shape[0]
    top_count = expert_ids.shape[1]
    exp_dev = w_gate_up.shape[0]
    hidden_units = w_down.shape[1]
    n_experts = exp_dev * lax.axis_size("attn") * lax.axis_size("exp")
    capacity = max(2, 2 * tok_rows * top_count // n_experts)
    flat_ids = expert_ids.reshape(-1)
    order = jnp.arange(flat_ids.shape[0], dtype=jnp.int32)
    earlier = (flat_ids[:, None] == flat_ids[None, :]) & (order[None, :] < order[:, None])
    slot = jnp.sum(earlier.astype(jnp.int32), -1)
    target = (flat_ids * capacity + slot).reshape(tok_rows, top_count)
    places = jnp.arange(n_experts * capacity, dtype=jnp.int32)
    placing = jnp.sum((places[:, None, None] == target[None, :, :]).astype(jnp.int32), -1).astype(
        jnp.bfloat16
    )
    sent = jnp.dot(placing, normed, preferred_element_type=jnp.float32).astype(jnp.bfloat16)
    sent = sent.reshape(n_experts, capacity, normed.shape[1])
    block = lax.all_to_all(sent, ("attn", "exp"), split_axis=0, concat_axis=0, tiled=True)
    n_src = block.shape[0] // exp_dev
    rows_four = block.reshape(n_src, exp_dev, block.shape[1], block.shape[2])
    both = jnp.einsum("sjmd,jdf->sjmf", rows_four, w_gate_up, preferred_element_type=jnp.float32)
    hidden = (jax.nn.silu(both[..., :hidden_units]) * both[..., hidden_units:]).astype(jnp.bfloat16)
    result = jnp.einsum("sjmf,jfd->sjmd", hidden, w_down, preferred_element_type=jnp.float32)
    result = result.astype(jnp.bfloat16).reshape(block.shape)
    returned = lax.all_to_all(result, ("attn", "exp"), split_axis=0, concat_axis=0, tiled=True)
    picked = (
        returned[flat_ids, slot].reshape(tok_rows, top_count, normed.shape[1]).astype(jnp.float32)
    )
    numer = gate_nums.astype(jnp.float32)
    weights = numer / jnp.sum(numer, -1, keepdims=True)
    return middle + jnp.sum(picked * weights[:, :, None], 1)


def fits_grid(mesh):
    return mesh.shape["groups"] == 2 and mesh.shape["attn"] == 4 and mesh.shape["exp"] == 4


def solution(mesh):
    in_specs = (
        P(("groups", "exp"), None, "attn"),
        P(("groups", "exp"), None, "attn"),
        P(("groups", "exp"), None, "attn"),
        P(("groups", "exp"), None, "attn"),
        P(("groups", "exp"), None, "attn"),
        P(("groups", "exp")),
        P("attn", "exp"),
        P(("groups", "exp", "attn"), None),
        P(),
        P(("groups", "exp", "attn"), None),
        P(("groups", "exp", "attn"), None),
        P(("attn", "exp"), None, None),
        P(("attn", "exp"), None, None),
    )
    out_specs = P(("groups", "exp", "attn"), None)
    body = grid_shards if fits_grid(mesh) else shards
    return jax.shard_map(body, mesh=mesh, in_specs=in_specs, out_specs=out_specs, check_vma=False)
```
